256 devices in a mesh: section: 4 (over y), band: 32 (over x, z), members: 2 (over core).
Axes of the slice: x: 4, y: 4, z: 8, core: 2. Of those that a mesh axis runs over, the one named last changes fastest.
Arguments:
- fields: bfloat16 [8, 128, 576, 128], P(('members', 'section'), 'band'), parts along dimension 0, may hold values from -6 to 6
- lat_taps: bfloat16 [2, 9, 128], replicated, may hold values from -1.5 to 1.5
- lon_taps: bfloat16 [2, 9, 128], replicated, may hold values from -1.5 to 1.5
- gains: float32 [2, 128], replicated, may hold values from 0.1 to 1.9
- w_in: bfloat16 [2, 128, 256], replicated, may hold values from -0.5 to 0.5
- w_out: bfloat16 [2, 256, 128], replicated, may hold values from -0.375 to 0.375
Outputs:
- final_states: bfloat16 [8, 128, 576, 128], P(('members', 'section'), 'band'), parts along dimension 0
The draws below stay inside these ranges and needn't reach their ends.
There are 2 independent parts, one for each index of `members`. The reference program is written for one: setup_inputs(seed, part) draws one part's arguments, and reference() takes and returns one part's arrays. A program takes and returns all parts, laid end to end along the dimension named above; an argument that names none is the same for every part. Nothing has to cross between parts.
All inputs are finite; a program needn't handle non-finite values.
Results may differ from the reference program's by a relative error of at most 0.0063.
Values may be sent and summed in bfloat16 or wider, within the bound.
A program may use at most 64 MiB of HBM per device.

```python
import jax
import jax.numpy as jnp
from jax import lax

C = 128
H = 256
LON = 576
DLON = 3
LAYERS = 2
MB = 4
LAT = 128


def shard_levels(rng, dims, split, low, largest):
    def one(axis_at, shards_of):
        heights = jax.random.uniform(jax.random.fold_in(jax.random.fold_in(rng, 6), axis_at), (shards_of,), jnp.float32, low / len(split), largest / len(split))
        return jnp.repeat(jnp.exp(heights), dims[axis_at] // shards_of).reshape((-1,) + (1,) * (len(dims) - axis_at - 1))

    factor_of = one(*split[0])
    for cut in split[1:]:
        factor_of = factor_of * one(*cut)
    return factor_of


def normal_values(rng, dims, deviation, most, split=(), dtype=jnp.bfloat16):
    level = shard_levels(rng, dims, split, -0.22, 0.18) if split else 1.0
    entries = jax.random.normal(rng, dims, jnp.float32) * deviation * level
    return jnp.minimum(jnp.maximum(entries, -most), most).astype(dtype)


def setup_inputs(seed: int = 0, part: int = 0) -> dict:
    key_of = jax.random.split(jax.random.key(seed), 7)
    part_splits = jax.random.split(jax.random.fold_in(key_of[6], part), 7)
    fields = normal_values(part_splits[0], (MB, LAT, LON, C), 1.0, 6.0, ((0, 4), (1, 32)))
    lat_taps = normal_values(key_of[1], (LAYERS, 9, C), 0.33, 1.5)
    lon_taps = normal_values(key_of[2], (LAYERS, 9, C), 0.33, 1.5)
    gains = jnp.clip(1.0 + 0.18 * jax.random.normal(key_of[3], (LAYERS, C), jnp.float32), 0.1, 1.9)
    w_in = normal_values(key_of[4], (LAYERS, C, H), C ** -0.5, 0.5)
    w_out = normal_values(key_of[5], (LAYERS, H, C), H ** -0.5, 0.375)
    return dict(fields=fields, lat_taps=lat_taps, lon_taps=lon_taps, gains=gains, w_in=w_in, w_out=w_out)


def layer_step(state, lat_w, lon_w, gain, proj_in, proj_out):
    rows = state.shape[0]
    wide = state.astype(jnp.float32)
    padded = jnp.pad(wide, ((4, 4), (0, 0), (0, 0)))
    lat_tap = lat_w.astype(jnp.float32)
    latmix = jnp.zeros_like(wide)
    for k in range(9):
        latmix = latmix + padded[k:k + rows] * lat_tap[k]
    latmix = latmix.astype(jnp.bfloat16).astype(jnp.float32)
    lon_tap = lon_w.astype(jnp.float32)
    lonmix = jnp.zeros_like(wide)
    for k in range(9):
        lonmix = lonmix + jnp.roll(latmix, -DLON * (k - 4), axis=1) * lon_tap[k]
    mean = lax.optimization_barrier(jnp.mean(lonmix, axis=-1, keepdims=True))
    centred = lonmix - mean
    var = lax.optimization_barrier(jnp.mean(centred * centred, axis=-1, keepdims=True))
    normed = (centred / jnp.sqrt(var + 1e-06) * gain).astype(jnp.bfloat16)
    flat = normed.reshape(-1, normed.shape[-1])
    hidden = jax.nn.gelu(jnp.dot(flat, proj_in, preferred_element_type=jnp.float32), approximate=False).astype(jnp.bfloat16)
    delta = jnp.dot(hidden, proj_out, preferred_element_type=jnp.float32).reshape(wide.shape)
    return (wide + delta).astype(jnp.bfloat16)

def reference(fields, lat_taps, lon_taps, gains, w_in, w_out):

    def run(state):
        for layer in range(LAYERS):
            state = layer_step(state, lat_taps[layer], lon_taps[layer], gains[layer], w_in[layer], w_out[layer])
        return state
    return lax.map(run, fields)
```

```python
import functools

import jax
import jax.numpy as jnp
from jax import lax
from jax.experimental import pallas as pl
from jax.experimental.pallas import tpu as pltpu
from jax.sharding import PartitionSpec as P

LAYERS = 2
TAPS = 9
REACH = 12
ROWS = 4
LON = 576
C = 128
H = 256
W = 48
N = LON // W
BANDS = 32
PAD = 16
MESH = pl.DeviceIdType.MESH


def kernel(fields, lat_taps, lon_taps, gains, w_in, w_out, out,
           state0, state1, mixed, result, lat16, lon16, lat32, lon32, gain32, win, wout,
           send_sem, recv_sem, load_sem, out_sem):
    band = lax.axis_index("band")
    has_up = band > 0
    has_down = band < BANDS - 1
    states = (state0, state1)

    barrier = pltpu.get_barrier_semaphore()

    @pl.when(has_up)
    def _():
        pl.semaphore_signal(barrier, inc=1, device_id={"band": band - 1}, device_id_type=MESH)

    @pl.when(has_down)
    def _():
        pl.semaphore_signal(barrier, inc=1, device_id={"band": band + 1}, device_id_type=MESH)

    loads = [
        pltpu.make_async_copy(fields.at[0], state0.at[ROWS:2 * ROWS, 0:LON], load_sem.at[0]),
        pltpu.make_async_copy(fields.at[0, :, 0:16], state0.at[ROWS:2 * ROWS, LON:LON + 16], load_sem.at[1]),
        pltpu.make_async_copy(lat_taps, lat16, load_sem.at[2]),
        pltpu.make_async_copy(lon_taps, lon16, load_sem.at[3]),
        pltpu.make_async_copy(gains, gain32, load_sem.at[4]),
        pltpu.make_async_copy(w_in, win, load_sem.at[5]),
        pltpu.make_async_copy(w_out, wout, load_sem.at[6]),
    ]
    for load in loads:
        load.start()

    def copy(layer, side, piece, start, width):
        place = states[layer]
        if layer == 0:
            source = fields.at[0, :, pl.ds(start, width)]
        else:
            source = place.at[ROWS:2 * ROWS, pl.ds(start, width)]
        first = 2 * ROWS if side == 0 else 0
        return pltpu.make_async_remote_copy(
            src_ref=source,
            dst_ref=place.at[first:first + ROWS, pl.ds(start, width)],
            send_sem=send_sem.at[layer, side, piece],
            recv_sem=recv_sem.at[layer, side, piece],
            device_id={"band": band - 1 if side == 0 else band + 1},
            device_id_type=MESH,
        )

    def send(layer, piece, start, width):
        @pl.when(has_up)
        def _():
            copy(layer, 0, piece, start, width).start()

        @pl.when(has_down)
        def _():
            copy(layer, 1, piece, start, width).start()

    def arrived(layer, piece, start, width):
        @pl.when(has_down)
        def _():
            copy(layer, 0, piece, start, width).wait_recv()

        @pl.when(has_up)
        def _():
            copy(layer, 1, piece, start, width).wait_recv()

    def sent(layer, piece, start, width):
        @pl.when(has_up)
        def _():
            copy(layer, 0, piece, start, width).wait_send()

        @pl.when(has_down)
        def _():
            copy(layer, 1, piece, start, width).wait_send()

    pl.semaphore_wait(barrier, has_up.astype(jnp.int32) + has_down.astype(jnp.int32))

    for piece in range(N):
        send(0, piece, piece * W, W)

    @pl.when(band == 0)
    def _():
        for place in states:
            place[0:ROWS] = jnp.zeros((ROWS,) + place.shape[1:], place.dtype)

    @pl.when(band == BANDS - 1)
    def _():
        for place in states:
            place[2 * ROWS:] = jnp.zeros((ROWS,) + place.shape[1:], place.dtype)

    for load in loads:
        load.wait()
    lat32[...] = lat16[...].astype(jnp.float32)
    lon32[...] = lon16[...].astype(jnp.float32)

    def latmix(layer, start, width):
        place = states[layer]
        for at in range(0, width, 16):
            rows = [place[r, pl.ds(start + at, 16), :].astype(jnp.float32) for r in range(3 * ROWS)]
            for i in range(ROWS):
                total = rows[i] * lat32[0, layer:layer + 1, :]
                for k in range(1, TAPS):
                    total = total + rows[i + k] * lat32[k, layer:layer + 1, :]
                mixed[layer, i, pl.ds(PAD + start + at, 16), :] = total.astype(jnp.bfloat16).astype(jnp.float32)

    def rest(layer, start, width, store, held=None):
        held = start if held is None else held
        for i in range(ROWS):
            total = mixed[layer, i, pl.ds(PAD + start - REACH, width), :] * lon32[0, layer:layer + 1, :]
            for k in range(1, TAPS):
                total = total + mixed[layer, i, pl.ds(PAD + start - REACH + 3 * k, width), :] * lon32[k, layer:layer + 1, :]
            mean = jnp.mean(total, axis=-1, keepdims=True)
            centred = total - mean
            var = jnp.mean(centred * centred, axis=-1, keepdims=True)
            normed = (centred * lax.rsqrt(var + 1e-06) * gain32[layer:layer + 1, :]).astype(jnp.bfloat16)
            inner = jnp.dot(normed, win[layer], preferred_element_type=jnp.float32)
            hidden = (0.5 * inner * (1.0 + lax.erf(inner * 0.7071067811865476))).astype(jnp.bfloat16)
            delta = jnp.dot(hidden, wout[layer], preferred_element_type=jnp.float32)
            old = states[layer][ROWS + i, pl.ds(held, width), :].astype(jnp.float32)
            store(i, (old + delta).astype(jnp.bfloat16))

    def keep(start, width):
        def store(i, value):
            state1[ROWS + i, pl.ds(start, width), :] = value
        return store

    def finish(start, width):
        def store(i, value):
            result[i, pl.ds(start, width), :] = value
        return store

    arrived(0, 0, 0, W)
    latmix(0, 0, W)
    for i in range(ROWS):
        mixed[0, i, PAD + LON:PAD + LON + W, :] = mixed[0, i, PAD:PAD + W, :]
    rest(0, 16, W - 32, keep(16, W - 32))
    send(1, 0, 16, W - 32)

    @pl.loop(1, N)
    def _(piece):
        start = pl.multiple_of(piece * W, 16)
        arrived(0, piece, start, W)
        latmix(0, start, W)
        rest(0, start - 16, W, keep(start - 16, W))
        send(1, piece, start - 16, W)

    rest(0, LON - 16, 32, keep(LON - 16, 32))
    send(1, N, LON - 16, 32)

    arrived(1, 0, 16, W - 32)
    latmix(1, 16, W - 32)

    @pl.loop(1, N)
    def _(piece):
        start = pl.multiple_of(piece * W, 16)
        arrived(1, piece, start - 16, W)
        latmix(1, start - 16, W)

        @pl.when(piece == 1)
        def _():
            for i in range(ROWS):
                mixed[1, i, PAD + LON + 16:PAD + LON + 48, :] = mixed[1, i, PAD + 16:PAD + 48, :]

        rest(1, start - 32, W, finish(start - 32, W))

    arrived(1, N, LON - 16, 32)
    latmix(1, LON - 16, 32)
    rest(1, LON - 32, 32, finish(LON - 32, 32))
    rest(1, LON, 16, finish(0, 16))
    rest(1, LON + 16, 16, finish(16, 16), held=16)

    written = pltpu.make_async_copy(result, out.at[0], out_sem)
    written.start()
    for piece in range(N):
        sent(0, piece, piece * W, W)
    sent(1, 0, 16, W - 32)
    for piece in range(1, N):
        sent(1, piece, piece * W - 16, W)
    sent(1, N, LON - 16, 32)
    written.wait()


def shards(fields, lat_taps, lon_taps, gains, w_in, w_out):
    return pl.pallas_call(
        kernel,
        out_shape=jax.ShapeDtypeStruct(fields.shape, fields.dtype),
        in_specs=[pl.BlockSpec(memory_space=pl.ANY)] * 6,
        out_specs=pl.BlockSpec(memory_space=pl.ANY),
        scratch_shapes=[
            pltpu.VMEM((3 * ROWS, LON + 16, C), jnp.bfloat16),
            pltpu.VMEM((3 * ROWS, LON + 16, C), jnp.bfloat16),
            pltpu.VMEM((LAYERS, ROWS, PAD + LON + 64, C), jnp.float32),
            pltpu.VMEM((ROWS, LON, C), jnp.bfloat16),
            pltpu.VMEM((TAPS, LAYERS, C), jnp.bfloat16),
            pltpu.VMEM((TAPS, LAYERS, C), jnp.bfloat16),
            pltpu.VMEM((TAPS, LAYERS, C), jnp.float32),
            pltpu.VMEM((TAPS, LAYERS, C), jnp.float32),
            pltpu.VMEM((LAYERS, C), jnp.float32),
            pltpu.VMEM((LAYERS, C, H), jnp.bfloat16),
            pltpu.VMEM((LAYERS, H, C), jnp.bfloat16),
            pltpu.SemaphoreType.DMA((LAYERS, 2, N + 1)),
            pltpu.SemaphoreType.DMA((LAYERS, 2, N + 1)),
            pltpu.SemaphoreType.DMA((7,)),
            pltpu.SemaphoreType.DMA,
        ],
        compiler_params=pltpu.CompilerParams(collective_id=0, has_side_effects=True),
        name="step",
    )(fields, jnp.transpose(lat_taps, (1, 0, 2)), jnp.transpose(lon_taps, (1, 0, 2)), gains, w_in, w_out)


def solution(mesh):
    return jax.shard_map(
        shards,
        mesh=mesh,
        in_specs=(P(("members", "section"), "band", None, None), P(), P(), P(), P(), P()),
        out_specs=P(("members", "section"), "band", None, None),
        check_vma=False,
    )
```

```python
import jax
import jax.numpy as jnp
from jax import lax
from jax.experimental import pallas as pl
from jax.experimental.pallas import tpu as pltpu
from jax.sharding import PartitionSpec as P

LAYERS = 2
TAPS = 9
REACH = 12
ROWS = 4
LON = 576
C = 128
H = 256
BANDS = 32
RUN = 8
PAD = 16
BLOCK = 48
MESH = pl.DeviceIdType.MESH

SENT = (
    ((0, 96), (96, 96), (192, 96), (288, 96), (384, 96), (480, 96)),
    ((16, 64), (80, 96), (176, 96), (272, 96), (368, 96), (464, 48), (512, 48), (560, 32)),
)
DONE = (
    ((16, 64), (80, 96), (176, 96), (272, 96), (368, 96), (464, 96)),
    ((32, 32), (64, 96), (160, 96), (256, 96), (352, 96), (448, 48), (496, 48), (544, 64)),
)
NEXT = ((0,), (1,), (2,), (3,), (4,), (5, 6))


def kernel(fields, lat_taps, lon_taps, gains, w_in, w_out, out,
           state0, state1, mixed, lat16, lon16, lat32, lon32, gain32, win, wout,
           send_sem, recv0_sem, recv1_sem, load_sem, ready_sem):
    band = lax.axis_index("band")
    place_in_run = lax.rem(band, RUN)
    opens = place_in_run == 0
    closes = place_in_run == RUN - 1
    has_up = band > 0
    has_down = band < BANDS - 1
    inside = jnp.logical_and(has_up, has_down)
    up_by_barrier = jnp.logical_and(has_up, jnp.logical_not(opens))
    up_by_ready = jnp.logical_and(has_up, opens)
    down_by_barrier = jnp.logical_and(has_down, closes)
    down_by_ready = jnp.logical_and(has_down, jnp.logical_not(closes))
    states = (state0, state1)
    recv_sems = (recv0_sem, recv1_sem)
    above, below = {"band": band - 1}, {"band": band + 1}

    barrier = pltpu.get_barrier_semaphore()

    @pl.when(down_by_ready)
    def _():
        pl.semaphore_signal(barrier, inc=1, device_id=below, device_id_type=MESH)

    @pl.when(up_by_ready)
    def _():
        pl.semaphore_signal(barrier, inc=1, device_id=above, device_id_type=MESH)

    own = pltpu.make_async_copy(fields.at[0], state0.at[ROWS:2 * ROWS, 0:LON], load_sem.at[0])
    loads = [
        pltpu.make_async_copy(lat_taps, lat16, load_sem.at[1]),
        pltpu.make_async_copy(lon_taps, lon16, load_sem.at[2]),
        pltpu.make_async_copy(gains, gain32, load_sem.at[3]),
        pltpu.make_async_copy(w_in, win, load_sem.at[4]),
        pltpu.make_async_copy(w_out, wout, load_sem.at[5]),
    ]
    own.start()
    for load in loads:
        load.start()

    def copy(layer, side, piece, sending=True):
        place = states[layer]
        start, width = SENT[layer][piece]
        first = 2 * ROWS if side == 0 else 0
        source = fields.at[0, :, start:start + width] if layer == 0 else place.at[ROWS:2 * ROWS, start:start + width]
        return pltpu.make_async_remote_copy(
            src_ref=source,
            dst_ref=place.at[first:first + ROWS, start:start + width],
            send_sem=send_sem.at[layer, side],
            recv_sem=recv_sems[layer].at[piece],
            device_id=above if side == 0 else below,
            device_id_type=MESH,
        )

    def send_side(layer, side, pieces):
        for piece in pieces:
            copy(layer, side, piece).start()

    def send(layer, pieces):
        @pl.when(has_up)
        def _():
            send_side(layer, 0, pieces)

        @pl.when(has_down)
        def _():
            send_side(layer, 1, pieces)

    def awaited(layer, piece, rows):
        start, width = SENT[layer][piece]
        part = states[layer].at[0:rows, start:start + width]
        return pltpu.make_async_remote_copy(
            src_ref=part, dst_ref=part, send_sem=send_sem.at[0, 0], recv_sem=recv_sems[layer].at[piece],
            device_id=above, device_id_type=MESH,
        )

    def arrived(layer, piece):
        @pl.when(inside)
        def _():
            awaited(layer, piece, 2 * ROWS).wait_recv()

        @pl.when(jnp.logical_not(inside))
        def _():
            awaited(layer, piece, ROWS).wait_recv()

    def sent(layer, side):
        start = SENT[layer][0][0]
        part = states[layer].at[0:ROWS, start:start + LON]
        pltpu.make_async_remote_copy(
            src_ref=part, dst_ref=part, send_sem=send_sem.at[layer, side], recv_sem=recv0_sem.at[0],
            device_id=above, device_id_type=MESH,
        ).wait_send()

    all_first = range(len(SENT[0]))

    @pl.when(jnp.logical_or(up_by_barrier, down_by_barrier))
    def _():
        pl.semaphore_wait(barrier, up_by_barrier.astype(jnp.int32) + down_by_barrier.astype(jnp.int32))

    @pl.when(up_by_barrier)
    def _():
        pl.semaphore_signal(ready_sem.at[0], inc=1, device_id=above, device_id_type=MESH)
        send_side(0, 0, all_first)

    @pl.when(down_by_barrier)
    def _():
        pl.semaphore_signal(ready_sem.at[1], inc=1, device_id=below, device_id_type=MESH)
        send_side(0, 1, all_first)

    @pl.when(down_by_ready)
    def _():
        pl.semaphore_wait(ready_sem.at[0], 1)
        send_side(0, 1, all_first)

    @pl.when(up_by_ready)
    def _():
        pl.semaphore_wait(ready_sem.at[1], 1)
        send_side(0, 0, all_first)

    @pl.when(jnp.logical_not(has_up))
    def _():
        for place in states:
            place[0:ROWS] = jnp.zeros((ROWS,) + place.shape[1:], place.dtype)

    @pl.when(jnp.logical_not(has_down))
    def _():
        for place in states:
            place[2 * ROWS:] = jnp.zeros((ROWS,) + place.shape[1:], place.dtype)

    own.wait()
    for load in loads:
        load.wait()
    state0[ROWS:2 * ROWS, LON:LON + 16, :] = state0[ROWS:2 * ROWS, 0:16, :]
    lat32[...] = lat16[...].astype(jnp.float32)
    lon32[...] = lon16[...].astype(jnp.float32)

    def latmix(layer, piece):
        place = states[layer]
        start, width = SENT[layer][piece]
        for at in range(start, start + width, 16):
            rows = [place[r, at:at + 16, :].astype(jnp.float32) for r in range(3 * ROWS)]
            for i in range(ROWS):
                total = rows[i] * lat32[0, layer:layer + 1, :]
                for k in range(1, TAPS):
                    total = total + rows[i + k] * lat32[k, layer:layer + 1, :]
                total = total.astype(jnp.bfloat16).astype(jnp.float32)
                mixed[layer, i, PAD + at:PAD + at + 16, :] = total
                if at + LON < (LAYERS + 1) * 16 + LON + layer * 16 - 16:
                    mixed[layer, i, PAD + at + LON:PAD + at + LON + 16, :] = total

    def rest(layer, start, width, store):
        totals = []
        for i in range(ROWS):
            at = PAD + start - REACH
            total = mixed[layer, i, at:at + width, :] * lon32[0, layer:layer + 1, :]
            for k in range(1, TAPS):
                total = total + mixed[layer, i, at + 3 * k:at + 3 * k + width, :] * lon32[k, layer:layer + 1, :]
            totals.append(total)
        total = jnp.concatenate(totals, axis=0)
        mean = jnp.mean(total, axis=-1, keepdims=True)
        centred = total - mean
        var = jnp.mean(centred * centred, axis=-1, keepdims=True)
        normed = (centred * lax.rsqrt(var + 1e-06) * gain32[layer:layer + 1, :]).astype(jnp.bfloat16)
        inner = jnp.dot(normed, win[layer], preferred_element_type=jnp.float32)
        hidden = (0.5 * inner * (1.0 + lax.erf(inner * 0.7071067811865476))).astype(jnp.bfloat16)
        delta = jnp.dot(hidden, wout[layer], preferred_element_type=jnp.float32)
        for i in range(ROWS):
            old = states[layer][ROWS + i, start:start + width, :].astype(jnp.float32)
            store(i, start, width, (old + delta[i * width:(i + 1) * width]).astype(jnp.bfloat16))

    def keep(i, start, width, value):
        state1[ROWS + i, start:start + width, :] = value
        if start == 16:
            state1[ROWS + i, LON + 16:LON + 32, :] = value[:16]

    def finish(i, start, width, value):
        if start + width <= LON:
            out[0, i, start:start + width, :] = value
        else:
            out[0, i, start:LON, :] = value[:LON - start]
            out[0, i, 0:start + width - LON, :] = value[LON - start:]

    def run(layer, start, width, store):
        for at in range(start, start + width, BLOCK):
            rest(layer, at, min(BLOCK, start + width - at), store)

    for piece in range(len(SENT[0])):
        arrived(0, piece)
        latmix(0, piece)
        run(0, *DONE[0][piece], keep)
        send(1, NEXT[piece])
    run(0, LON - 16, 32, keep)
    send(1, (len(SENT[1]) - 1,))

    for piece in range(len(SENT[1])):
        arrived(1, piece)
        latmix(1, piece)
        if piece < len(SENT[1]) - 1:
            run(1, *DONE[1][piece], finish)
        else:
            rest(1, *DONE[1][piece], finish)

    for layer in range(LAYERS):
        @pl.when(has_up)
        def _():
            sent(layer, 0)

        @pl.when(has_down)
        def _():
            sent(layer, 1)


def shards(fields, lat_taps, lon_taps, gains, w_in, w_out):
    return pl.pallas_call(
        kernel,
        out_shape=pltpu.VMEM(fields.shape, fields.dtype),
        in_specs=[pl.BlockSpec(memory_space=pl.ANY)] * 6,
        out_specs=pl.BlockSpec(memory_space=pltpu.VMEM),
        scratch_shapes=[
            pltpu.VMEM((3 * ROWS, LON + 32, C), jnp.bfloat16),
            pltpu.VMEM((3 * ROWS, LON + 32, C), jnp.bfloat16),
            pltpu.VMEM((LAYERS, ROWS, PAD + LON + 64, C), jnp.float32),
            pltpu.VMEM((TAPS, LAYERS, C), jnp.bfloat16),
            pltpu.VMEM((TAPS, LAYERS, C), jnp.bfloat16),
            pltpu.VMEM((TAPS, LAYERS, C), jnp.float32),
            pltpu.VMEM((TAPS, LAYERS, C), jnp.float32),
            pltpu.VMEM((LAYERS, C), jnp.float32),
            pltpu.VMEM((LAYERS, C, H), jnp.bfloat16),
            pltpu.VMEM((LAYERS, H, C), jnp.bfloat16),
            pltpu.SemaphoreType.DMA((LAYERS, 2)),
            pltpu.SemaphoreType.DMA((len(SENT[0]),)),
            pltpu.SemaphoreType.DMA((len(SENT[1]),)),
            pltpu.SemaphoreType.DMA((6,)),
            pltpu.SemaphoreType.REGULAR((2,)),
        ],
        compiler_params=pltpu.CompilerParams(collective_id=0, has_side_effects=True),
        name="step",
    )(fields, jnp.transpose(lat_taps, (1, 0, 2)), jnp.transpose(lon_taps, (1, 0, 2)), gains, w_in, w_out)


def solution(mesh):
    return jax.shard_map(
        shards,
        mesh=mesh,
        in_specs=(P(("members", "section"), "band", None, None), P(), P(), P(), P(), P()),
        out_specs=P(("members", "section"), "band", None, None),
        check_vma=False,
    )
```

```python
import jax
import jax.numpy as jnp
from jax import lax
from jax.experimental import pallas as pl
from jax.experimental.pallas import tpu as pltpu
from jax.sharding import PartitionSpec as P

LAYERS = 2
TAPS = 9
REACH = 12
ROWS = 4
LON = 576
C = 128
H = 256
BANDS = 32
RUN = 8
PAD = 16
BLOCK = 48
MESH = pl.DeviceIdType.MESH

SENT = (
    ((0, 96), (96, 96), (192, 96), (288, 96), (384, 96), (480, 96)),
    ((16, 64), (80, 96), (176, 96), (272, 96), (368, 96), (464, 48), (512, 48), (560, 32)),
)
DONE = (
    ((16, 64), (80, 96), (176, 96), (272, 96), (368, 96), (464, 96)),
    ((32, 32), (64, 96), (160, 96), (256, 96), (352, 96), (448, 48), (496, 48), (544, 64)),
)
RELAYED = ((3, 4, 5), (0, 1, 2))
NEXT = ((0,), (1,), (2,), (3,), (4,), (5, 6))


def kernel(fields, lat_taps, lon_taps, gains, w_in, w_out, out,
           state0, state1, mixed, lat16, lon16, lat32, lon32, gain32, win, wout,
           relay0, relay1, send_sem, recv0_sem, recv1_sem, load_sem, ready_sem, relay_sem):
    band = lax.axis_index("band")
    place_in_run = lax.rem(band, RUN)
    run_index = band // RUN
    opens = place_in_run == 0
    closes = place_in_run == RUN - 1
    has_up = band > 0
    has_down = band < BANDS - 1
    inside = jnp.logical_and(has_up, has_down)
    up_by_barrier = jnp.logical_and(has_up, jnp.logical_not(opens))
    up_by_ready = jnp.logical_and(has_up, opens)
    down_by_barrier = jnp.logical_and(has_down, closes)
    down_by_ready = jnp.logical_and(has_down, jnp.logical_not(closes))
    states = (state0, state1)
    recv_sems = (recv0_sem, recv1_sem)
    above, below = {"band": band - 1}, {"band": band + 1}
    run_before, run_after = {"band": band - RUN}, {"band": band + RUN}
    run_start, run_end = {"band": band - (RUN - 1)}, {"band": band + (RUN - 1)}
    relays = (relay0, relay1)
    later, sooner = run_index > 0, run_index < BANDS // RUN - 1
    by_run_after = jnp.logical_and(closes, sooner)
    by_run_before = jnp.logical_and(opens, later)
    passes_down = jnp.logical_and(closes, later)
    passes_up = jnp.logical_and(opens, sooner)

    def down_count(run):
        return run + 1

    def up_count(run):
        return BANDS // RUN - run

    def is_relayed(layer, slot, count):
        return count >= (len(RELAYED[0]) - slot if layer == 0 else slot + 1)

    barrier = pltpu.get_barrier_semaphore()

    @pl.when(down_by_ready)
    def _():
        pl.semaphore_signal(barrier, inc=1, device_id=below, device_id_type=MESH)

    @pl.when(up_by_ready)
    def _():
        pl.semaphore_signal(barrier, inc=1, device_id=above, device_id_type=MESH)

    @pl.when(opens)
    def _():
        pl.semaphore_signal(barrier, inc=1, device_id=run_end, device_id_type=MESH)

    @pl.when(jnp.logical_and(sooner, jnp.logical_or(opens, closes)))
    def _():
        pl.semaphore_signal(barrier, inc=1, device_id=run_after, device_id_type=MESH)

    own = pltpu.make_async_copy(fields.at[0], state0.at[ROWS:2 * ROWS, 0:LON], load_sem.at[0])
    loads = [
        pltpu.make_async_copy(lat_taps, lat16, load_sem.at[1]),
        pltpu.make_async_copy(lon_taps, lon16, load_sem.at[2]),
        pltpu.make_async_copy(gains, gain32, load_sem.at[3]),
        pltpu.make_async_copy(w_in, win, load_sem.at[4]),
        pltpu.make_async_copy(w_out, wout, load_sem.at[5]),
    ]
    own.start()
    for load in loads:
        load.start()

    def copy(layer, side, piece, sending=True):
        place = states[layer]
        start, width = SENT[layer][piece]
        first = 2 * ROWS if side == 0 else 0
        source = fields.at[0, :, start:start + width] if layer == 0 else place.at[ROWS:2 * ROWS, start:start + width]
        return pltpu.make_async_remote_copy(
            src_ref=source,
            dst_ref=place.at[first:first + ROWS, start:start + width],
            send_sem=send_sem.at[layer, side],
            recv_sem=recv_sems[layer].at[piece],
            device_id=above if side == 0 else below,
            device_id_type=MESH,
        )

    def slot_of(layer, piece):
        return layer * len(RELAYED[0]) + RELAYED[layer].index(piece)

    def detour(layer, side, piece):
        start, width = SENT[layer][piece]
        source = fields.at[0, :, start:start + width] if layer == 0 else state1.at[ROWS:2 * ROWS, start:start + width]
        return pltpu.make_async_remote_copy(
            src_ref=source,
            dst_ref=relays[layer].at[:, start:start + width],
            send_sem=send_sem.at[layer, side],
            recv_sem=relay_sem.at[slot_of(layer, piece)],
            device_id=run_before if side == 0 else run_after,
            device_id_type=MESH,
        )

    def onward(layer, side, piece):
        start, width = SENT[layer][piece]
        first = 2 * ROWS if side == 0 else 0
        return pltpu.make_async_remote_copy(
            src_ref=relays[layer].at[:, start:start + width],
            dst_ref=states[layer].at[first:first + ROWS, start:start + width],
            send_sem=relay_sem.at[slot_of(layer, piece)],
            recv_sem=recv_sems[layer].at[piece],
            device_id=run_end if side == 0 else run_start,
            device_id_type=MESH,
        )

    def goes_round(layer, side, piece):
        if piece not in RELAYED[layer] or (layer == 1 and side == 0):
            return None
        slot = RELAYED[layer].index(piece)
        if side == 0:
            return jnp.logical_and(by_run_before, is_relayed(layer, slot, up_count(run_index)))
        return jnp.logical_and(by_run_after, is_relayed(layer, slot, down_count(run_index)))

    def send_direct(layer, side, pieces):
        for piece in pieces:
            round_about = goes_round(layer, side, piece)
            if round_about is None:
                copy(layer, side, piece).start()
            else:
                @pl.when(jnp.logical_not(round_about))
                def _():
                    copy(layer, side, piece).start()

    def send_round(layer, side, pieces):
        for piece in pieces:
            round_about = goes_round(layer, side, piece)
            if round_about is not None:
                @pl.when(round_about)
                def _():
                    detour(layer, side, piece).start()

    def send(layer, pieces):
        @pl.when(has_up)
        def _():
            send_direct(layer, 0, pieces)

        @pl.when(has_down)
        def _():
            send_direct(layer, 1, pieces)

        send_round(layer, 1, pieces)

    def passed(layer, side, piece):
        slot = RELAYED[layer].index(piece)
        if side == 0:
            return jnp.logical_and(passes_up, is_relayed(layer, slot, up_count(run_index + 1)))
        return jnp.logical_and(passes_down, is_relayed(layer, slot, down_count(run_index - 1)))

    def pass_on(layer, side, piece):
        @pl.when(passed(layer, side, piece))
        def _():
            start, width = SENT[layer][piece]
            part = relays[layer].at[:, start:start + width]
            pltpu.make_async_remote_copy(
                src_ref=part, dst_ref=part, send_sem=send_sem.at[0, 0], recv_sem=relay_sem.at[slot_of(layer, piece)],
                device_id=above, device_id_type=MESH,
            ).wait_recv()
            onward(layer, side, piece).start()

    def passed_on(layer, side, piece):
        @pl.when(passed(layer, side, piece))
        def _():
            onward(layer, side, piece).wait_send()

    def awaited(layer, piece, rows):
        start, width = SENT[layer][piece]
        part = states[layer].at[0:rows, start:start + width]
        return pltpu.make_async_remote_copy(
            src_ref=part, dst_ref=part, send_sem=send_sem.at[0, 0], recv_sem=recv_sems[layer].at[piece],
            device_id=above, device_id_type=MESH,
        )

    def arrived(layer, piece):
        @pl.when(inside)
        def _():
            awaited(layer, piece, 2 * ROWS).wait_recv()

        @pl.when(jnp.logical_not(inside))
        def _():
            awaited(layer, piece, ROWS).wait_recv()

    def sent(layer, side):
        start = SENT[layer][0][0]
        part = states[layer].at[0:ROWS, start:start + LON]
        pltpu.make_async_remote_copy(
            src_ref=part, dst_ref=part, send_sem=send_sem.at[layer, side], recv_sem=recv0_sem.at[0],
            device_id=above, device_id_type=MESH,
        ).wait_send()

    all_first = range(len(SENT[0]))
    first_in_all = jnp.logical_and(opens, jnp.logical_not(later))

    @pl.when(jnp.logical_not(first_in_all))
    def _():
        pl.semaphore_wait(
            barrier,
            up_by_barrier.astype(jnp.int32) + down_by_barrier.astype(jnp.int32) + closes.astype(jnp.int32)
            + passes_down.astype(jnp.int32) + by_run_before.astype(jnp.int32),
        )

    @pl.when(down_by_barrier)
    def _():
        pl.semaphore_signal(ready_sem.at[1], inc=1, device_id=below, device_id_type=MESH)
        send_direct(0, 1, all_first)

    @pl.when(up_by_barrier)
    def _():
        pl.semaphore_signal(ready_sem.at[0], inc=1, device_id=above, device_id_type=MESH)
        send_direct(0, 0, all_first)

    @pl.when(passes_down)
    def _():
        pl.semaphore_signal(ready_sem.at[2], inc=1, device_id=run_before, device_id_type=MESH)

    @pl.when(by_run_after)
    def _():
        pl.semaphore_signal(ready_sem.at[3], inc=1, device_id=run_start, device_id_type=MESH)
        pl.semaphore_wait(ready_sem.at[2], 1)

    send_round(0, 1, all_first)
    send_round(0, 0, all_first)

    @pl.when(down_by_ready)
    def _():
        pl.semaphore_wait(ready_sem.at[0], 1)
        send_direct(0, 1, all_first)

    @pl.when(up_by_ready)
    def _():
        pl.semaphore_wait(ready_sem.at[1], 1)
        send_direct(0, 0, all_first)

    @pl.when(passes_up)
    def _():
        pl.semaphore_wait(ready_sem.at[3], 1)

    @pl.when(jnp.logical_not(has_up))
    def _():
        for place in states:
            place[0:ROWS] = jnp.zeros((ROWS,) + place.shape[1:], place.dtype)

    @pl.when(jnp.logical_not(has_down))
    def _():
        for place in states:
            place[2 * ROWS:] = jnp.zeros((ROWS,) + place.shape[1:], place.dtype)

    own.wait()
    for load in loads:
        load.wait()
    state0[ROWS:2 * ROWS, LON:LON + 16, :] = state0[ROWS:2 * ROWS, 0:16, :]
    lat32[...] = lat16[...].astype(jnp.float32)
    lon32[...] = lon16[...].astype(jnp.float32)

    def latmix(layer, piece):
        place = states[layer]
        start, width = SENT[layer][piece]
        for at in range(start, start + width, 16):
            rows = [place[r, at:at + 16, :].astype(jnp.float32) for r in range(3 * ROWS)]
            for i in range(ROWS):
                total = rows[i] * lat32[0, layer:layer + 1, :]
                for k in range(1, TAPS):
                    total = total + rows[i + k] * lat32[k, layer:layer + 1, :]
                total = total.astype(jnp.bfloat16).astype(jnp.float32)
                mixed[layer, i, PAD + at:PAD + at + 16, :] = total
                if at + LON < (LAYERS + 1) * 16 + LON + layer * 16 - 16:
                    mixed[layer, i, PAD + at + LON:PAD + at + LON + 16, :] = total

    def rest(layer, start, width, store):
        totals = []
        for i in range(ROWS):
            at = PAD + start - REACH
            total = mixed[layer, i, at:at + width, :] * lon32[0, layer:layer + 1, :]
            for k in range(1, TAPS):
                total = total + mixed[layer, i, at + 3 * k:at + 3 * k + width, :] * lon32[k, layer:layer + 1, :]
            totals.append(total)
        total = jnp.concatenate(totals, axis=0)
        mean = jnp.mean(total, axis=-1, keepdims=True)
        centred = total - mean
        var = jnp.mean(centred * centred, axis=-1, keepdims=True)
        normed = (centred * lax.rsqrt(var + 1e-06) * gain32[layer:layer + 1, :]).astype(jnp.bfloat16)
        inner = jnp.dot(normed, win[layer], preferred_element_type=jnp.float32)
        hidden = (0.5 * inner * (1.0 + lax.erf(inner * 0.7071067811865476))).astype(jnp.bfloat16)
        delta = jnp.dot(hidden, wout[layer], preferred_element_type=jnp.float32)
        for i in range(ROWS):
            old = states[layer][ROWS + i, start:start + width, :].astype(jnp.float32)
            store(i, start, width, (old + delta[i * width:(i + 1) * width]).astype(jnp.bfloat16))

    def keep(i, start, width, value):
        state1[ROWS + i, start:start + width, :] = value
        if start == 16:
            state1[ROWS + i, LON + 16:LON + 32, :] = value[:16]

    def finish(i, start, width, value):
        if start + width <= LON:
            out[0, i, start:start + width, :] = value
        else:
            out[0, i, start:LON, :] = value[:LON - start]
            out[0, i, 0:start + width - LON, :] = value[LON - start:]

    def run(layer, start, width, store):
        for at in range(start, start + width, BLOCK):
            rest(layer, at, min(BLOCK, start + width - at), store)

    for piece in range(len(SENT[0])):
        if piece < 3:
            pass_on(0, 0, RELAYED[0][piece])
            pass_on(0, 1, RELAYED[0][piece])
        else:
            pass_on(1, 1, RELAYED[1][piece - 3])
        arrived(0, piece)
        latmix(0, piece)
        run(0, *DONE[0][piece], keep)
        send(1, NEXT[piece])
    run(0, LON - 16, 32, keep)
    send(1, (len(SENT[1]) - 1,))

    for piece in range(len(SENT[1])):
        arrived(1, piece)
        latmix(1, piece)
        if piece < len(SENT[1]) - 1:
            run(1, *DONE[1][piece], finish)
        else:
            rest(1, *DONE[1][piece], finish)

    for slot in range(3):
        passed_on(0, 0, RELAYED[0][slot])
        passed_on(0, 1, RELAYED[0][slot])
        passed_on(1, 1, RELAYED[1][slot])
    for layer in range(LAYERS):
        @pl.when(has_up)
        def _():
            sent(layer, 0)

        @pl.when(has_down)
        def _():
            sent(layer, 1)


def shards(fields, lat_taps, lon_taps, gains, w_in, w_out):
    return pl.pallas_call(
        kernel,
        out_shape=pltpu.VMEM(fields.shape, fields.dtype),
        in_specs=[pl.BlockSpec(memory_space=pl.ANY)] * 6,
        out_specs=pl.BlockSpec(memory_space=pltpu.VMEM),
        scratch_shapes=[
            pltpu.VMEM((3 * ROWS, LON + 32, C), jnp.bfloat16),
            pltpu.VMEM((3 * ROWS, LON + 32, C), jnp.bfloat16),
            pltpu.VMEM((LAYERS, ROWS, PAD + LON + 64, C), jnp.float32),
            pltpu.VMEM((TAPS, LAYERS, C), jnp.bfloat16),
            pltpu.VMEM((TAPS, LAYERS, C), jnp.bfloat16),
            pltpu.VMEM((TAPS, LAYERS, C), jnp.float32),
            pltpu.VMEM((TAPS, LAYERS, C), jnp.float32),
            pltpu.VMEM((LAYERS, C), jnp.float32),
            pltpu.VMEM((LAYERS, C, H), jnp.bfloat16),
            pltpu.VMEM((LAYERS, H, C), jnp.bfloat16),
            pltpu.VMEM((ROWS, LON, C), jnp.bfloat16),
            pltpu.VMEM((ROWS, LON, C), jnp.bfloat16),
            pltpu.SemaphoreType.DMA((LAYERS, 2)),
            pltpu.SemaphoreType.DMA((len(SENT[0]),)),
            pltpu.SemaphoreType.DMA((len(SENT[1]),)),
            pltpu.SemaphoreType.DMA((6,)),
            pltpu.SemaphoreType.REGULAR((4,)),
            pltpu.SemaphoreType.DMA((6,)),
        ],
        compiler_params=pltpu.CompilerParams(collective_id=0, has_side_effects=True),
        name="step",
    )(fields, jnp.transpose(lat_taps, (1, 0, 2)), jnp.transpose(lon_taps, (1, 0, 2)), gains, w_in, w_out)


def solution(mesh):
    return jax.shard_map(
        shards,
        mesh=mesh,
        in_specs=(P(("members", "section"), "band", None, None), P(), P(), P(), P(), P()),
        out_specs=P(("members", "section"), "band", None, None),
        check_vma=False,
    )
```

```python
import jax
import jax.numpy as jnp
from jax import lax
from jax.experimental import pallas as pl
from jax.experimental.pallas import tpu as pltpu
from jax.sharding import PartitionSpec as P

LAYERS = 2
TAPS = 9
REACH = 12
ROWS = 4
LON = 576
C = 128
H = 256
BANDS = 32
RUN = 8
PAD = 16
BLOCK = 48
MESH = pl.DeviceIdType.MESH

SENT = (
    ((0, 96), (96, 96), (192, 96), (288, 96), (384, 96), (480, 96)),
    ((16, 64), (80, 96), (176, 96), (272, 96), (368, 96), (464, 48), (512, 48), (560, 32)),
)
DONE = (
    ((16, 64), (80, 96), (176, 96), (272, 96), (368, 96), (464, 96)),
    ((32, 32), (64, 96), (160, 96), (256, 96), (352, 96), (448, 48), (496, 48), (544, 64)),
)
RELAYED = ((3, 4, 5), (0, 1, 2))
NEXT = ((0,), (1,), (2,), (3,), (4,), (5, 6))


def kernel(fields, lat_taps, lon_taps, gains, w_in, w_out, out,
           state0, state1, mixed, lat16, lon16, lat32, lon32, gain32, win, wout,
           relay0, relay1, send_sem, recv0_sem, recv1_sem, load_sem, ready_sem, relay_sem):
    band = lax.axis_index("band")
    place_in_run = lax.rem(band, RUN)
    run_index = band // RUN
    opens = place_in_run == 0
    closes = place_in_run == RUN - 1
    has_up = band > 0
    has_down = band < BANDS - 1
    inside = jnp.logical_and(has_up, has_down)
    down_by_ready = jnp.logical_and(has_down, jnp.logical_not(closes))
    states = (state0, state1)
    recv_sems = (recv0_sem, recv1_sem)
    above, below = {"band": band - 1}, {"band": band + 1}
    run_before, run_after = {"band": band - RUN}, {"band": band + RUN}
    run_start, run_end = {"band": band - (RUN - 1)}, {"band": band + (RUN - 1)}
    relays = (relay0, relay1)
    later, sooner = run_index > 0, run_index < BANDS // RUN - 1
    sends_round = jnp.logical_and(closes, sooner)
    passes = jnp.logical_and(closes, later)
    greeted_late = jnp.logical_and(opens, later)

    def is_relayed(layer, slot, count):
        return count >= (len(RELAYED[0]) - slot if layer == 0 else slot + 1)

    barrier = pltpu.get_barrier_semaphore()

    @pl.when(down_by_ready)
    def _():
        pl.semaphore_signal(barrier, inc=1, device_id=below, device_id_type=MESH)

    @pl.when(sends_round)
    def _():
        pl.semaphore_signal(barrier, inc=1, device_id=below, device_id_type=MESH)
        pl.semaphore_signal(barrier, inc=1, device_id=run_after, device_id_type=MESH)

    @pl.when(greeted_late)
    def _():
        pl.semaphore_signal(barrier, inc=1, device_id=above, device_id_type=MESH)
        pl.semaphore_signal(barrier, inc=1, device_id=run_end, device_id_type=MESH)

    own = pltpu.make_async_copy(fields.at[0], state0.at[ROWS:2 * ROWS, 0:LON], load_sem.at[0])
    loads = [
        pltpu.make_async_copy(lat_taps, lat16, load_sem.at[1]),
        pltpu.make_async_copy(lon_taps, lon16, load_sem.at[2]),
        pltpu.make_async_copy(gains, gain32, load_sem.at[3]),
        pltpu.make_async_copy(w_in, win, load_sem.at[4]),
        pltpu.make_async_copy(w_out, wout, load_sem.at[5]),
    ]
    own.start()
    for load in loads:
        load.start()

    def copy(layer, side, piece, sending=True):
        place = states[layer]
        start, width = SENT[layer][piece]
        first = 2 * ROWS if side == 0 else 0
        source = fields.at[0, :, start:start + width] if layer == 0 else place.at[ROWS:2 * ROWS, start:start + width]
        return pltpu.make_async_remote_copy(
            src_ref=source,
            dst_ref=place.at[first:first + ROWS, start:start + width],
            send_sem=send_sem.at[layer, side],
            recv_sem=recv_sems[layer].at[piece],
            device_id=above if side == 0 else below,
            device_id_type=MESH,
        )

    def slot_of(layer, piece):
        return layer * len(RELAYED[0]) + RELAYED[layer].index(piece)

    def detour(layer, piece):
        start, width = SENT[layer][piece]
        source = fields.at[0, :, start:start + width] if layer == 0 else state1.at[ROWS:2 * ROWS, start:start + width]
        return pltpu.make_async_remote_copy(
            src_ref=source,
            dst_ref=relays[layer].at[:, start:start + width],
            send_sem=send_sem.at[layer, 1],
            recv_sem=relay_sem.at[slot_of(layer, piece)],
            device_id=run_after,
            device_id_type=MESH,
        )

    def onward(layer, piece):
        start, width = SENT[layer][piece]
        return pltpu.make_async_remote_copy(
            src_ref=relays[layer].at[:, start:start + width],
            dst_ref=states[layer].at[0:ROWS, start:start + width],
            send_sem=relay_sem.at[slot_of(layer, piece)],
            recv_sem=recv_sems[layer].at[piece],
            device_id=run_start,
            device_id_type=MESH,
        )

    def goes_round(layer, piece):
        return jnp.logical_and(sends_round, is_relayed(layer, RELAYED[layer].index(piece), run_index + 1))

    def send_up(layer, pieces):
        for piece in pieces:
            copy(layer, 0, piece).start()

    def send_down(layer, pieces):
        for piece in pieces:
            if piece not in RELAYED[layer]:
                copy(layer, 1, piece).start()
            else:
                @pl.when(jnp.logical_not(goes_round(layer, piece)))
                def _():
                    copy(layer, 1, piece).start()

    def send_round(layer, pieces):
        for piece in pieces:
            if piece in RELAYED[layer]:
                @pl.when(goes_round(layer, piece))
                def _():
                    detour(layer, piece).start()

    def send(layer, pieces):
        send_round(layer, pieces)

        @pl.when(has_down)
        def _():
            send_down(layer, pieces)

        @pl.when(has_up)
        def _():
            send_up(layer, pieces)

    def passed(layer, piece):
        return jnp.logical_and(passes, is_relayed(layer, RELAYED[layer].index(piece), run_index))

    def pass_on(layer, piece):
        @pl.when(passed(layer, piece))
        def _():
            start, width = SENT[layer][piece]
            part = relays[layer].at[:, start:start + width]
            pltpu.make_async_remote_copy(
                src_ref=part, dst_ref=part, send_sem=send_sem.at[0, 0], recv_sem=relay_sem.at[slot_of(layer, piece)],
                device_id=above, device_id_type=MESH,
            ).wait_recv()
            onward(layer, piece).start()

    def passed_on(layer, piece):
        @pl.when(passed(layer, piece))
        def _():
            onward(layer, piece).wait_send()

    def awaited(layer, piece, rows):
        start, width = SENT[layer][piece]
        part = states[layer].at[0:rows, start:start + width]
        return pltpu.make_async_remote_copy(
            src_ref=part, dst_ref=part, send_sem=send_sem.at[0, 0], recv_sem=recv_sems[layer].at[piece],
            device_id=above, device_id_type=MESH,
        )

    def arrived(layer, piece):
        @pl.when(inside)
        def _():
            awaited(layer, piece, 2 * ROWS).wait_recv()

        @pl.when(jnp.logical_not(inside))
        def _():
            awaited(layer, piece, ROWS).wait_recv()

    def sent(layer, side):
        start = SENT[layer][0][0]
        part = states[layer].at[0:ROWS, start:start + LON]
        pltpu.make_async_remote_copy(
            src_ref=part, dst_ref=part, send_sem=send_sem.at[layer, side], recv_sem=recv0_sem.at[0],
            device_id=above, device_id_type=MESH,
        ).wait_send()

    all_first = range(len(SENT[0]))

    @pl.when(jnp.logical_not(opens))
    def _():
        pl.semaphore_wait(barrier, 1 + sends_round.astype(jnp.int32) + 2 * passes.astype(jnp.int32))
        pl.semaphore_signal(ready_sem.at[0], inc=1, device_id=above, device_id_type=MESH)

    @pl.when(passes)
    def _():
        pl.semaphore_signal(ready_sem.at[1], inc=1, device_id=run_before, device_id_type=MESH)

    @pl.when(sends_round)
    def _():
        send_down(0, all_first)

    @pl.when(jnp.logical_not(opens))
    def _():
        send_up(0, all_first)

    @pl.when(sends_round)
    def _():
        pl.semaphore_wait(ready_sem.at[1], 1)
        send_round(0, all_first)

    @pl.when(down_by_ready)
    def _():
        pl.semaphore_wait(ready_sem.at[0], 1)
        send_down(0, all_first)

    @pl.when(greeted_late)
    def _():
        pl.semaphore_wait(barrier, 1)
        send_up(0, all_first)

    @pl.when(jnp.logical_not(has_up))
    def _():
        for place in states:
            place[0:ROWS] = jnp.zeros((ROWS,) + place.shape[1:], place.dtype)

    @pl.when(jnp.logical_not(has_down))
    def _():
        for place in states:
            place[2 * ROWS:] = jnp.zeros((ROWS,) + place.shape[1:], place.dtype)

    own.wait()
    for load in loads:
        load.wait()
    state0[ROWS:2 * ROWS, LON:LON + 16, :] = state0[ROWS:2 * ROWS, 0:16, :]
    lat32[...] = lat16[...].astype(jnp.float32)
    lon32[...] = lon16[...].astype(jnp.float32)

    def latmix(layer, piece):
        place = states[layer]
        start, width = SENT[layer][piece]
        for at in range(start, start + width, 16):
            rows = [place[r, at:at + 16, :].astype(jnp.float32) for r in range(3 * ROWS)]
            for i in range(ROWS):
                total = rows[i] * lat32[0, layer:layer + 1, :]
                for k in range(1, TAPS):
                    total = total + rows[i + k] * lat32[k, layer:layer + 1, :]
                total = total.astype(jnp.bfloat16).astype(jnp.float32)
                mixed[layer, i, PAD + at:PAD + at + 16, :] = total
                if at + LON < (LAYERS + 1) * 16 + LON + layer * 16 - 16:
                    mixed[layer, i, PAD + at + LON:PAD + at + LON + 16, :] = total

    def rest(layer, start, width, store):
        totals = []
        for i in range(ROWS):
            at = PAD + start - REACH
            total = mixed[layer, i, at:at + width, :] * lon32[0, layer:layer + 1, :]
            for k in range(1, TAPS):
                total = total + mixed[layer, i, at + 3 * k:at + 3 * k + width, :] * lon32[k, layer:layer + 1, :]
            totals.append(total)
        total = jnp.concatenate(totals, axis=0)
        mean = jnp.mean(total, axis=-1, keepdims=True)
        centred = total - mean
        var = jnp.mean(centred * centred, axis=-1, keepdims=True)
        normed = (centred * lax.rsqrt(var + 1e-06) * gain32[layer:layer + 1, :]).astype(jnp.bfloat16)
        inner = jnp.dot(normed, win[layer], preferred_element_type=jnp.float32)
        hidden = (0.5 * inner * (1.0 + lax.erf(inner * 0.7071067811865476))).astype(jnp.bfloat16)
        delta = jnp.dot(hidden, wout[layer], preferred_element_type=jnp.float32)
        for i in range(ROWS):
            old = states[layer][ROWS + i, start:start + width, :].astype(jnp.float32)
            store(i, start, width, (old + delta[i * width:(i + 1) * width]).astype(jnp.bfloat16))

    def keep(i, start, width, value):
        state1[ROWS + i, start:start + width, :] = value
        if start == 16:
            state1[ROWS + i, LON + 16:LON + 32, :] = value[:16]

    def finish(i, start, width, value):
        if start + width <= LON:
            out[0, i, start:start + width, :] = value
        else:
            out[0, i, start:LON, :] = value[:LON - start]
            out[0, i, 0:start + width - LON, :] = value[LON - start:]

    def run(layer, start, width, store):
        for at in range(start, start + width, BLOCK):
            rest(layer, at, min(BLOCK, start + width - at), store)

    for piece in range(len(SENT[0])):
        if piece < 3:
            pass_on(0, RELAYED[0][piece])
        else:
            pass_on(1, RELAYED[1][piece - 3])
        arrived(0, piece)
        latmix(0, piece)
        run(0, *DONE[0][piece], keep)
        send(1, NEXT[piece])
    run(0, LON - 16, 32, keep)
    send(1, (len(SENT[1]) - 1,))

    for piece in range(len(SENT[1])):
        arrived(1, piece)
        latmix(1, piece)
        if piece < len(SENT[1]) - 1:
            run(1, *DONE[1][piece], finish)
        else:
            rest(1, *DONE[1][piece], finish)

    for slot in range(3):
        passed_on(0, RELAYED[0][slot])
        passed_on(1, RELAYED[1][slot])
    for layer in range(LAYERS):
        @pl.when(has_up)
        def _():
            sent(layer, 0)

        @pl.when(has_down)
        def _():
            sent(layer, 1)


def shards(fields, lat_taps, lon_taps, gains, w_in, w_out):
    return pl.pallas_call(
        kernel,
        out_shape=pltpu.VMEM(fields.shape, fields.dtype),
        in_specs=[pl.BlockSpec(memory_space=pl.ANY)] * 6,
        out_specs=pl.BlockSpec(memory_space=pltpu.VMEM),
        scratch_shapes=[
            pltpu.VMEM((3 * ROWS, LON + 32, C), jnp.bfloat16),
            pltpu.VMEM((3 * ROWS, LON + 32, C), jnp.bfloat16),
            pltpu.VMEM((LAYERS, ROWS, PAD + LON + 64, C), jnp.float32),
            pltpu.VMEM((TAPS, LAYERS, C), jnp.bfloat16),
            pltpu.VMEM((TAPS, LAYERS, C), jnp.bfloat16),
            pltpu.VMEM((TAPS, LAYERS, C), jnp.float32),
            pltpu.VMEM((TAPS, LAYERS, C), jnp.float32),
            pltpu.VMEM((LAYERS, C), jnp.float32),
            pltpu.VMEM((LAYERS, C, H), jnp.bfloat16),
            pltpu.VMEM((LAYERS, H, C), jnp.bfloat16),
            pltpu.VMEM((ROWS, LON, C), jnp.bfloat16),
            pltpu.VMEM((ROWS, LON, C), jnp.bfloat16),
            pltpu.SemaphoreType.DMA((LAYERS, 2)),
            pltpu.SemaphoreType.DMA((len(SENT[0]),)),
            pltpu.SemaphoreType.DMA((len(SENT[1]),)),
            pltpu.SemaphoreType.DMA((6,)),
            pltpu.SemaphoreType.REGULAR((2,)),
            pltpu.SemaphoreType.DMA((6,)),
        ],
        compiler_params=pltpu.CompilerParams(collective_id=0, has_side_effects=True),
        name="step",
    )(fields, jnp.transpose(lat_taps, (1, 0, 2)), jnp.transpose(lon_taps, (1, 0, 2)), gains, w_in, w_out)


def solution(mesh):
    return jax.shard_map(
        shards,
        mesh=mesh,
        in_specs=(P(("members", "section"), "band", None, None), P(), P(), P(), P(), P()),
        out_specs=P(("members", "section"), "band", None, None),
        check_vma=False,
    )
```

```python
import jax
import jax.numpy as jnp
from jax import lax
from jax.experimental import pallas as pl
from jax.experimental.pallas import tpu as pltpu
from jax.sharding import PartitionSpec as P

LAYERS = 2
TAPS = 9
REACH = 12
ROWS = 4
LON = 576
C = 128
H = 256
BANDS = 32
RUN = 8
RUNS = BANDS // RUN
PAD = 16
BLOCK = 48
MESH = pl.DeviceIdType.MESH

SENT = (
    ((0, 96), (96, 96), (192, 96), (288, 96), (384, 96), (480, 96)),
    ((16, 64), (80, 96), (176, 96), (272, 96), (368, 96), (464, 48), (512, 48), (560, 32)),
)
DONE = (
    ((16, 64), (80, 96), (176, 96), (272, 96), (368, 96), (464, 96)),
    ((32, 32), (64, 96), (160, 96), (256, 96), (352, 96), (448, 48), (496, 48), (544, 64)),
)
RELAYED = ((3, 4, 5), (0, 1, 2))
NEXT = ((0,), (1,), (2,), (3,), (4,), (5, 6))


def kernel(fields, lat_taps, lon_taps, gains, w_in, w_out, out,
           state0, state1, mixed, lat16, lon16, lat32, lon32, gain32, win, wout,
           relay0, relay1, send_sem, recv0_sem, recv1_sem, load_sem, ready_sem, relay_sem):
    band = lax.axis_index("band")
    place_in_run = lax.rem(band, RUN)
    run_index = band // RUN
    opens = place_in_run == 0
    closes = place_in_run == RUN - 1
    has_up = band > 0
    has_down = band < BANDS - 1
    inside = jnp.logical_and(has_up, has_down)
    tied_above = place_in_run >= RUN - 2
    tied_below = jnp.logical_and(place_in_run >= RUN - 3, jnp.logical_not(closes))
    states = (state0, state1)
    recv_sems = (recv0_sem, recv1_sem)
    above, below = {"band": band - 1}, {"band": band + 1}
    run_before, run_after = {"band": band - RUN}, {"band": band + RUN}
    run_start, run_end = {"band": band - (RUN - 1)}, {"band": band + (RUN - 1)}
    relays = (relay0, relay1)
    later, sooner = run_index > 0, run_index < RUNS - 1
    round_down = jnp.logical_and(closes, sooner)
    round_up = jnp.logical_and(opens, later)
    passes_down = jnp.logical_and(closes, later)
    passes_up = jnp.logical_and(opens, sooner)

    def is_relayed(layer, slot, count):
        return count >= (len(RELAYED[0]) - slot if layer == 0 else slot + 1)

    barrier = pltpu.get_barrier_semaphore()

    def greet(condition, device):
        @pl.when(condition)
        def _():
            pl.semaphore_signal(barrier, inc=1, device_id=device, device_id_type=MESH)

    greet(jnp.logical_or(place_in_run < RUN - 2, round_down), below)
    greet(jnp.logical_or(tied_above, round_up), above)
    greet(opens, run_end)
    greet(jnp.logical_or(round_down, passes_up), run_after)

    own = pltpu.make_async_copy(fields.at[0], state0.at[ROWS:2 * ROWS, 0:LON], load_sem.at[0])
    loads = [
        pltpu.make_async_copy(lat_taps, lat16, load_sem.at[1]),
        pltpu.make_async_copy(lon_taps, lon16, load_sem.at[2]),
        pltpu.make_async_copy(gains, gain32, load_sem.at[3]),
        pltpu.make_async_copy(w_in, win, load_sem.at[4]),
        pltpu.make_async_copy(w_out, wout, load_sem.at[5]),
    ]
    own.start()
    for load in loads:
        load.start()

    def copy(layer, side, piece, sending=True):
        place = states[layer]
        start, width = SENT[layer][piece]
        first = 2 * ROWS if side == 0 else 0
        source = fields.at[0, :, start:start + width] if layer == 0 else place.at[ROWS:2 * ROWS, start:start + width]
        return pltpu.make_async_remote_copy(
            src_ref=source,
            dst_ref=place.at[first:first + ROWS, start:start + width],
            send_sem=send_sem.at[layer, side],
            recv_sem=recv_sems[layer].at[piece],
            device_id=above if side == 0 else below,
            device_id_type=MESH,
        )

    def slot_of(layer, piece):
        return layer * len(RELAYED[0]) + RELAYED[layer].index(piece)

    def detour(layer, side, piece):
        start, width = SENT[layer][piece]
        source = fields.at[0, :, start:start + width] if layer == 0 else state1.at[ROWS:2 * ROWS, start:start + width]
        return pltpu.make_async_remote_copy(
            src_ref=source,
            dst_ref=relays[layer].at[:, start:start + width],
            send_sem=send_sem.at[layer, side],
            recv_sem=relay_sem.at[slot_of(layer, piece)],
            device_id=run_before if side == 0 else run_after,
            device_id_type=MESH,
        )

    def onward(layer, side, piece):
        start, width = SENT[layer][piece]
        first = 2 * ROWS if side == 0 else 0
        return pltpu.make_async_remote_copy(
            src_ref=relays[layer].at[:, start:start + width],
            dst_ref=states[layer].at[first:first + ROWS, start:start + width],
            send_sem=relay_sem.at[slot_of(layer, piece)],
            recv_sem=recv_sems[layer].at[piece],
            device_id=run_end if side == 0 else run_start,
            device_id_type=MESH,
        )

    def goes_round(layer, side, piece):
        if piece not in RELAYED[layer] or (layer == 1 and side == 0):
            return None
        slot = RELAYED[layer].index(piece)
        if side == 0:
            return jnp.logical_and(round_up, is_relayed(layer, slot, RUNS - run_index))
        return jnp.logical_and(round_down, is_relayed(layer, slot, run_index + 1))

    def send_direct(layer, side, pieces):
        for piece in pieces:
            round_about = goes_round(layer, side, piece)
            if round_about is None:
                copy(layer, side, piece).start()
            else:
                @pl.when(jnp.logical_not(round_about))
                def _():
                    copy(layer, side, piece).start()

    def send_up(layer, pieces):
        send_direct(layer, 0, pieces)

    def send_down(layer, pieces):
        send_direct(layer, 1, pieces)

    def send_round(layer, side, pieces):
        for piece in pieces:
            round_about = goes_round(layer, side, piece)
            if round_about is not None:
                @pl.when(round_about)
                def _():
                    detour(layer, side, piece).start()

    def send(layer, pieces):
        send_round(layer, 1, pieces)

        @pl.when(has_down)
        def _():
            send_down(layer, pieces)

        @pl.when(has_up)
        def _():
            send_up(layer, pieces)

    def passed(layer, side, piece):
        slot = RELAYED[layer].index(piece)
        if side == 0:
            return jnp.logical_and(passes_up, is_relayed(layer, slot, RUNS - 1 - run_index))
        return jnp.logical_and(passes_down, is_relayed(layer, slot, run_index))

    def pass_on(layer, side, piece):
        @pl.when(passed(layer, side, piece))
        def _():
            start, width = SENT[layer][piece]
            part = relays[layer].at[:, start:start + width]
            pltpu.make_async_remote_copy(
                src_ref=part, dst_ref=part, send_sem=send_sem.at[0, 0], recv_sem=relay_sem.at[slot_of(layer, piece)],
                device_id=above, device_id_type=MESH,
            ).wait_recv()
            onward(layer, side, piece).start()

    def passed_on(layer, side, piece):
        @pl.when(passed(layer, side, piece))
        def _():
            onward(layer, side, piece).wait_send()

    def awaited(layer, piece, rows):
        start, width = SENT[layer][piece]
        part = states[layer].at[0:rows, start:start + width]
        return pltpu.make_async_remote_copy(
            src_ref=part, dst_ref=part, send_sem=send_sem.at[0, 0], recv_sem=recv_sems[layer].at[piece],
            device_id=above, device_id_type=MESH,
        )

    def arrived(layer, piece):
        @pl.when(inside)
        def _():
            awaited(layer, piece, 2 * ROWS).wait_recv()

        @pl.when(jnp.logical_not(inside))
        def _():
            awaited(layer, piece, ROWS).wait_recv()

    def sent(layer, side):
        start = SENT[layer][0][0]
        part = states[layer].at[0:ROWS, start:start + LON]
        pltpu.make_async_remote_copy(
            src_ref=part, dst_ref=part, send_sem=send_sem.at[layer, side], recv_sem=recv0_sem.at[0],
            device_id=above, device_id_type=MESH,
        ).wait_send()

    all_first = range(len(SENT[0]))

    def answer(condition, which, device):
        @pl.when(condition)
        def _():
            pl.semaphore_signal(ready_sem.at[which], inc=1, device_id=device, device_id_type=MESH)

    @pl.when(jnp.logical_not(opens))
    def _():
        pl.semaphore_wait(barrier, 1 + (tied_below | round_down).astype(jnp.int32) + passes_down.astype(jnp.int32))

    @pl.when(tied_below | round_down)
    def _():
        send_down(0, all_first)

    answer(passes_down, 1, run_before)
    answer(round_down, 1, run_start)
    answer(jnp.logical_and(place_in_run > 0, place_in_run < RUN - 2), 0, above)
    answer(place_in_run == RUN - 2, 0, below)

    @pl.when(jnp.logical_not(opens | closes))
    def _():
        send_up(0, all_first)

    @pl.when(round_down)
    def _():
        pl.semaphore_wait(ready_sem.at[1], 1)
        send_round(0, 1, all_first)

    @pl.when(jnp.logical_not(tied_below))
    def _():
        pl.semaphore_wait(ready_sem.at[0], 1)

        @pl.when(closes)
        def _():
            send_up(0, all_first)

        @pl.when(jnp.logical_not(closes))
        def _():
            send_down(0, all_first)

    @pl.when(round_up)
    def _():
        pl.semaphore_wait(barrier, 2)
        send_up(0, all_first)
        send_round(0, 0, all_first)

    @pl.when(passes_up)
    def _():
        pl.semaphore_wait(ready_sem.at[1], 1)

    @pl.when(jnp.logical_not(has_up))
    def _():
        for place in states:
            place[0:ROWS] = jnp.zeros((ROWS,) + place.shape[1:], place.dtype)

    @pl.when(jnp.logical_not(has_down))
    def _():
        for place in states:
            place[2 * ROWS:] = jnp.zeros((ROWS,) + place.shape[1:], place.dtype)

    own.wait()
    for load in loads:
        load.wait()
    state0[ROWS:2 * ROWS, LON:LON + 16, :] = state0[ROWS:2 * ROWS, 0:16, :]
    lat32[...] = lat16[...].astype(jnp.float32)
    lon32[...] = lon16[...].astype(jnp.float32)

    def latmix(layer, piece):
        place = states[layer]
        start, width = SENT[layer][piece]
        for at in range(start, start + width, 16):
            rows = [place[r, at:at + 16, :].astype(jnp.float32) for r in range(3 * ROWS)]
            for i in range(ROWS):
                total = rows[i] * lat32[0, layer:layer + 1, :]
                for k in range(1, TAPS):
                    total = total + rows[i + k] * lat32[k, layer:layer + 1, :]
                total = total.astype(jnp.bfloat16).astype(jnp.float32)
                mixed[layer, i, PAD + at:PAD + at + 16, :] = total
                if at + LON < (LAYERS + 1) * 16 + LON + layer * 16 - 16:
                    mixed[layer, i, PAD + at + LON:PAD + at + LON + 16, :] = total

    def rest(layer, start, width, store):
        totals = []
        for i in range(ROWS):
            at = PAD + start - REACH
            total = mixed[layer, i, at:at + width, :] * lon32[0, layer:layer + 1, :]
            for k in range(1, TAPS):
                total = total + mixed[layer, i, at + 3 * k:at + 3 * k + width, :] * lon32[k, layer:layer + 1, :]
            totals.append(total)
        total = jnp.concatenate(totals, axis=0)
        mean = jnp.mean(total, axis=-1, keepdims=True)
        centred = total - mean
        var = jnp.mean(centred * centred, axis=-1, keepdims=True)
        normed = (centred * lax.rsqrt(var + 1e-06) * gain32[layer:layer + 1, :]).astype(jnp.bfloat16)
        inner = jnp.dot(normed, win[layer], preferred_element_type=jnp.float32)
        hidden = (0.5 * inner * (1.0 + lax.erf(inner * 0.7071067811865476))).astype(jnp.bfloat16)
        delta = jnp.dot(hidden, wout[layer], preferred_element_type=jnp.float32)
        for i in range(ROWS):
            old = states[layer][ROWS + i, start:start + width, :].astype(jnp.float32)
            store(i, start, width, (old + delta[i * width:(i + 1) * width]).astype(jnp.bfloat16))

    def keep(i, start, width, value):
        state1[ROWS + i, start:start + width, :] = value
        if start == 16:
            state1[ROWS + i, LON + 16:LON + 32, :] = value[:16]

    def finish(i, start, width, value):
        if start + width <= LON:
            out[0, i, start:start + width, :] = value
        else:
            out[0, i, start:LON, :] = value[:LON - start]
            out[0, i, 0:start + width - LON, :] = value[LON - start:]

    def run(layer, start, width, store):
        for at in range(start, start + width, BLOCK):
            rest(layer, at, min(BLOCK, start + width - at), store)

    for piece in range(len(SENT[0])):
        if piece < 3:
            pass_on(0, 1, RELAYED[0][piece])
            pass_on(0, 0, RELAYED[0][piece])
        arrived(0, piece)
        latmix(0, piece)
        run(0, *DONE[0][piece], keep)
        if piece in (2, 3, 4):
            pass_on(1, 1, RELAYED[1][piece - 2])
        send(1, NEXT[piece])
    run(0, LON - 16, 32, keep)
    send(1, (len(SENT[1]) - 1,))

    for piece in range(len(SENT[1])):
        arrived(1, piece)
        latmix(1, piece)
        if piece < len(SENT[1]) - 1:
            run(1, *DONE[1][piece], finish)
        else:
            rest(1, *DONE[1][piece], finish)

    for slot in range(3):
        passed_on(0, 0, RELAYED[0][slot])
        passed_on(0, 1, RELAYED[0][slot])
        passed_on(1, 1, RELAYED[1][slot])
    for layer in range(LAYERS):
        @pl.when(has_up)
        def _():
            sent(layer, 0)

        @pl.when(has_down)
        def _():
            sent(layer, 1)


def shards(fields, lat_taps, lon_taps, gains, w_in, w_out):
    return pl.pallas_call(
        kernel,
        out_shape=pltpu.VMEM(fields.shape, fields.dtype),
        in_specs=[pl.BlockSpec(memory_space=pl.ANY)] * 6,
        out_specs=pl.BlockSpec(memory_space=pltpu.VMEM),
        scratch_shapes=[
            pltpu.VMEM((3 * ROWS, LON + 32, C), jnp.bfloat16),
            pltpu.VMEM((3 * ROWS, LON + 32, C), jnp.bfloat16),
            pltpu.VMEM((LAYERS, ROWS, PAD + LON + 64, C), jnp.float32),
            pltpu.VMEM((TAPS, LAYERS, C), jnp.bfloat16),
            pltpu.VMEM((TAPS, LAYERS, C), jnp.bfloat16),
            pltpu.VMEM((TAPS, LAYERS, C), jnp.float32),
            pltpu.VMEM((TAPS, LAYERS, C), jnp.float32),
            pltpu.VMEM((LAYERS, C), jnp.float32),
            pltpu.VMEM((LAYERS, C, H), jnp.bfloat16),
            pltpu.VMEM((LAYERS, H, C), jnp.bfloat16),
            pltpu.VMEM((ROWS, LON, C), jnp.bfloat16),
            pltpu.VMEM((ROWS, LON, C), jnp.bfloat16),
            pltpu.SemaphoreType.DMA((LAYERS, 2)),
            pltpu.SemaphoreType.DMA((len(SENT[0]),)),
            pltpu.SemaphoreType.DMA((len(SENT[1]),)),
            pltpu.SemaphoreType.DMA((6,)),
            pltpu.SemaphoreType.REGULAR((2,)),
            pltpu.SemaphoreType.DMA((6,)),
        ],
        compiler_params=pltpu.CompilerParams(collective_id=0, has_side_effects=True),
        name="step",
    )(fields, jnp.transpose(lat_taps, (1, 0, 2)), jnp.transpose(lon_taps, (1, 0, 2)), gains, w_in, w_out)


def solution(mesh):
    return jax.shard_map(
        shards,
        mesh=mesh,
        in_specs=(P(("members", "section"), "band", None, None), P(), P(), P(), P(), P()),
        out_specs=P(("members", "section"), "band", None, None),
        check_vma=False,
    )
```

```python
import jax
import jax.numpy as jnp
from jax import lax
from jax.experimental import pallas as pl
from jax.experimental.pallas import tpu as pltpu
from jax.sharding import PartitionSpec as P

LAYERS = 2
TAPS = 9
REACH = 12
ROWS = 4
LON = 576
C = 128
H = 256
BANDS = 32
RUN = 8
RUNS = BANDS // RUN
PAD = 16
BLOCK = 48
MESH = pl.DeviceIdType.MESH

SENT = (
    ((0, 96), (96, 96), (192, 96), (288, 96), (384, 96), (480, 96)),
    ((16, 64), (80, 96), (176, 96), (272, 96), (368, 96), (464, 64), (528, 64)),
)
DONE = (
    ((16, 64), (80, 96), (176, 96), (272, 96), (368, 96), (464, 96)),
    ((32, 32), (64, 96), (160, 96), (256, 96), (352, 96), (448, 64), (512, 96)),
)
RELAYED = ((3, 4, 5), (0, 1, 2))
NEXT = ((0,), (1,), (2,), (3,), (4,), (5,))


def kernel(fields, lat_taps, lon_taps, gains, w_in, w_out, out,
           state0, state1, mixed, lat16, lon16, lat32, lon32, gain32, win, wout,
           relay0, relay1, send_sem, recv0_sem, recv1_sem, load_sem, ready_sem, relay_sem):
    band = lax.axis_index("band")
    place_in_run = lax.rem(band, RUN)
    run_index = band // RUN
    opens = place_in_run == 0
    closes = place_in_run == RUN - 1
    has_up = band > 0
    has_down = band < BANDS - 1
    inside = jnp.logical_and(has_up, has_down)
    tied_above = place_in_run >= RUN - 2
    tied_below = jnp.logical_and(place_in_run >= RUN - 3, jnp.logical_not(closes))
    states = (state0, state1)
    recv_sems = (recv0_sem, recv1_sem)
    above, below = {"band": band - 1}, {"band": band + 1}
    run_before, run_after = {"band": band - RUN}, {"band": band + RUN}
    run_start, run_end = {"band": band - (RUN - 1)}, {"band": band + (RUN - 1)}
    relays = (relay0, relay1)
    later, sooner = run_index > 0, run_index < RUNS - 1
    round_down = jnp.logical_and(closes, sooner)
    round_up = jnp.logical_and(opens, later)
    passes_down = jnp.logical_and(closes, later)
    passes_up = jnp.logical_and(opens, sooner)

    def is_relayed(layer, slot, count):
        return count >= (len(RELAYED[0]) - slot if layer == 0 else slot + 1)

    barrier = pltpu.get_barrier_semaphore()

    def greet(condition, device):
        @pl.when(condition)
        def _():
            pl.semaphore_signal(barrier, inc=1, device_id=device, device_id_type=MESH)

    greet(jnp.logical_or(place_in_run < RUN - 2, round_down), below)
    greet(jnp.logical_or(tied_above, round_up), above)
    greet(opens, run_end)
    greet(jnp.logical_or(round_down, passes_up), run_after)

    own = pltpu.make_async_copy(fields.at[0], state0.at[ROWS:2 * ROWS, 0:LON], load_sem.at[0])
    loads = [
        pltpu.make_async_copy(lat_taps, lat16, load_sem.at[1]),
        pltpu.make_async_copy(lon_taps, lon16, load_sem.at[2]),
        pltpu.make_async_copy(gains, gain32, load_sem.at[3]),
        pltpu.make_async_copy(w_in, win, load_sem.at[4]),
        pltpu.make_async_copy(w_out, wout, load_sem.at[5]),
    ]
    own.start()
    for load in loads:
        load.start()

    def copy(layer, side, piece, sending=True):
        place = states[layer]
        start, width = SENT[layer][piece]
        first = 2 * ROWS if side == 0 else 0
        source = fields.at[0, :, start:start + width] if layer == 0 else place.at[ROWS:2 * ROWS, start:start + width]
        return pltpu.make_async_remote_copy(
            src_ref=source,
            dst_ref=place.at[first:first + ROWS, start:start + width],
            send_sem=send_sem.at[layer, side],
            recv_sem=recv_sems[layer].at[piece],
            device_id=above if side == 0 else below,
            device_id_type=MESH,
        )

    def slot_of(layer, piece):
        return layer * len(RELAYED[0]) + RELAYED[layer].index(piece)

    def detour(layer, side, piece):
        start, width = SENT[layer][piece]
        source = fields.at[0, :, start:start + width] if layer == 0 else state1.at[ROWS:2 * ROWS, start:start + width]
        return pltpu.make_async_remote_copy(
            src_ref=source,
            dst_ref=relays[layer].at[:, start:start + width],
            send_sem=send_sem.at[layer, side],
            recv_sem=relay_sem.at[slot_of(layer, piece)],
            device_id=run_before if side == 0 else run_after,
            device_id_type=MESH,
        )

    def onward(layer, side, piece):
        start, width = SENT[layer][piece]
        first = 2 * ROWS if side == 0 else 0
        return pltpu.make_async_remote_copy(
            src_ref=relays[layer].at[:, start:start + width],
            dst_ref=states[layer].at[first:first + ROWS, start:start + width],
            send_sem=relay_sem.at[slot_of(layer, piece)],
            recv_sem=recv_sems[layer].at[piece],
            device_id=run_end if side == 0 else run_start,
            device_id_type=MESH,
        )

    def goes_round(layer, side, piece):
        if piece not in RELAYED[layer] or (layer == 1 and side == 0):
            return None
        slot = RELAYED[layer].index(piece)
        if side == 0:
            return jnp.logical_and(round_up, is_relayed(layer, slot, RUNS - run_index))
        return jnp.logical_and(round_down, is_relayed(layer, slot, run_index + 1))

    def send_direct(layer, side, pieces):
        for piece in pieces:
            round_about = goes_round(layer, side, piece)
            if round_about is None:
                copy(layer, side, piece).start()
            else:
                @pl.when(jnp.logical_not(round_about))
                def _():
                    copy(layer, side, piece).start()

    def send_up(layer, pieces):
        send_direct(layer, 0, pieces)

    def send_down(layer, pieces):
        send_direct(layer, 1, pieces)

    def send_round(layer, side, pieces):
        for piece in pieces:
            round_about = goes_round(layer, side, piece)
            if round_about is not None:
                @pl.when(round_about)
                def _():
                    detour(layer, side, piece).start()

    def send(layer, pieces):
        send_round(layer, 1, pieces)

        @pl.when(has_down)
        def _():
            send_down(layer, pieces)

        @pl.when(has_up)
        def _():
            send_up(layer, pieces)

    def passed(layer, side, piece):
        slot = RELAYED[layer].index(piece)
        if side == 0:
            return jnp.logical_and(passes_up, is_relayed(layer, slot, RUNS - 1 - run_index))
        return jnp.logical_and(passes_down, is_relayed(layer, slot, run_index))

    def pass_on(layer, side, piece):
        @pl.when(passed(layer, side, piece))
        def _():
            start, width = SENT[layer][piece]
            part = relays[layer].at[:, start:start + width]
            pltpu.make_async_remote_copy(
                src_ref=part, dst_ref=part, send_sem=send_sem.at[0, 0], recv_sem=relay_sem.at[slot_of(layer, piece)],
                device_id=above, device_id_type=MESH,
            ).wait_recv()
            onward(layer, side, piece).start()

    def passed_on(layer, side, piece):
        @pl.when(passed(layer, side, piece))
        def _():
            onward(layer, side, piece).wait_send()

    def awaited(layer, piece, rows):
        start, width = SENT[layer][piece]
        part = states[layer].at[0:rows, start:start + width]
        return pltpu.make_async_remote_copy(
            src_ref=part, dst_ref=part, send_sem=send_sem.at[0, 0], recv_sem=recv_sems[layer].at[piece],
            device_id=above, device_id_type=MESH,
        )

    def arrived(layer, piece):
        @pl.when(inside)
        def _():
            awaited(layer, piece, 2 * ROWS).wait_recv()

        @pl.when(jnp.logical_not(inside))
        def _():
            awaited(layer, piece, ROWS).wait_recv()

    def sent(layer, side):
        start = SENT[layer][0][0]
        part = states[layer].at[0:ROWS, start:start + LON]
        pltpu.make_async_remote_copy(
            src_ref=part, dst_ref=part, send_sem=send_sem.at[layer, side], recv_sem=recv0_sem.at[0],
            device_id=above, device_id_type=MESH,
        ).wait_send()

    all_first = range(len(SENT[0]))

    def answer(condition, which, device):
        @pl.when(condition)
        def _():
            pl.semaphore_signal(ready_sem.at[which], inc=1, device_id=device, device_id_type=MESH)

    @pl.when(jnp.logical_not(opens))
    def _():
        pl.semaphore_wait(barrier, 1 + (tied_below | round_down).astype(jnp.int32) + passes_down.astype(jnp.int32))

    @pl.when(tied_below | round_down)
    def _():
        send_down(0, all_first)

    answer(passes_down, 1, run_before)
    answer(round_down, 1, run_start)
    answer(jnp.logical_and(place_in_run > 0, place_in_run < RUN - 2), 0, above)
    answer(place_in_run == RUN - 2, 0, below)

    @pl.when(jnp.logical_not(opens | closes))
    def _():
        send_up(0, all_first)

    @pl.when(round_down)
    def _():
        pl.semaphore_wait(ready_sem.at[1], 1)
        send_round(0, 1, all_first)

    @pl.when(jnp.logical_not(tied_below))
    def _():
        pl.semaphore_wait(ready_sem.at[0], 1)

        @pl.when(closes)
        def _():
            send_up(0, all_first)

        @pl.when(jnp.logical_not(closes))
        def _():
            send_down(0, all_first)

    @pl.when(round_up)
    def _():
        pl.semaphore_wait(barrier, 2)
        send_up(0, all_first)
        send_round(0, 0, all_first)

    @pl.when(passes_up)
    def _():
        pl.semaphore_wait(ready_sem.at[1], 1)

    @pl.when(jnp.logical_not(has_up))
    def _():
        for place in states:
            place[0:ROWS] = jnp.zeros((ROWS,) + place.shape[1:], place.dtype)

    @pl.when(jnp.logical_not(has_down))
    def _():
        for place in states:
            place[2 * ROWS:] = jnp.zeros((ROWS,) + place.shape[1:], place.dtype)

    own.wait()
    for load in loads:
        load.wait()
    state0[ROWS:2 * ROWS, LON:LON + 16, :] = state0[ROWS:2 * ROWS, 0:16, :]
    lat32[...] = lat16[...].astype(jnp.float32)
    lon32[...] = lon16[...].astype(jnp.float32)

    def latmix(layer, piece):
        place = states[layer]
        start, width = SENT[layer][piece]
        for at in range(start, start + width, 16):
            rows = [place[r, at:at + 16, :].astype(jnp.float32) for r in range(3 * ROWS)]
            for i in range(ROWS):
                total = rows[i] * lat32[0, layer:layer + 1, :]
                for k in range(1, TAPS):
                    total = total + rows[i + k] * lat32[k, layer:layer + 1, :]
                total = total.astype(jnp.bfloat16).astype(jnp.float32)
                mixed[layer, i, PAD + at:PAD + at + 16, :] = total
                if at + LON < (LAYERS + 1) * 16 + LON + layer * 16 - 16:
                    mixed[layer, i, PAD + at + LON:PAD + at + LON + 16, :] = total

    def rest(layer, start, width, store):
        totals = []
        for i in range(ROWS):
            at = PAD + start - REACH
            total = mixed[layer, i, at:at + width, :] * lon32[0, layer:layer + 1, :]
            for k in range(1, TAPS):
                total = total + mixed[layer, i, at + 3 * k:at + 3 * k + width, :] * lon32[k, layer:layer + 1, :]
            totals.append(total)
        total = jnp.concatenate(totals, axis=0)
        mean = jnp.mean(total, axis=-1, keepdims=True)
        centred = total - mean
        var = jnp.mean(centred * centred, axis=-1, keepdims=True)
        normed = (centred * lax.rsqrt(var + 1e-06) * gain32[layer:layer + 1, :]).astype(jnp.bfloat16)
        inner = jnp.dot(normed, win[layer], preferred_element_type=jnp.float32)
        hidden = (0.5 * inner * (1.0 + lax.erf(inner * 0.7071067811865476))).astype(jnp.bfloat16)
        delta = jnp.dot(hidden, wout[layer], preferred_element_type=jnp.float32)
        for i in range(ROWS):
            old = states[layer][ROWS + i, start:start + width, :].astype(jnp.float32)
            store(i, start, width, (old + delta[i * width:(i + 1) * width]).astype(jnp.bfloat16))

    def keep(i, start, width, value):
        state1[ROWS + i, start:start + width, :] = value
        if start == 16:
            state1[ROWS + i, LON + 16:LON + 32, :] = value[:16]

    def finish(i, start, width, value):
        if start + width <= LON:
            out[0, i, start:start + width, :] = value
        else:
            out[0, i, start:LON, :] = value[:LON - start]
            out[0, i, 0:start + width - LON, :] = value[LON - start:]

    def run(layer, start, width, store):
        for at in range(start, start + width, BLOCK):
            rest(layer, at, min(BLOCK, start + width - at), store)

    for piece in range(len(SENT[0])):
        if piece < 3:
            pass_on(0, 1, RELAYED[0][piece])
            pass_on(0, 0, RELAYED[0][piece])
        arrived(0, piece)
        latmix(0, piece)
        run(0, *DONE[0][piece], keep)
        if piece in (2, 3, 4):
            pass_on(1, 1, RELAYED[1][piece - 2])
        send(1, NEXT[piece])
    run(0, LON - 16, 32, keep)
    send(1, (len(SENT[1]) - 1,))

    for piece in range(len(SENT[1])):
        arrived(1, piece)
        latmix(1, piece)
        run(1, *DONE[1][piece], finish)

    for slot in range(3):
        passed_on(0, 0, RELAYED[0][slot])
        passed_on(0, 1, RELAYED[0][slot])
        passed_on(1, 1, RELAYED[1][slot])
    for layer in range(LAYERS):
        @pl.when(has_up)
        def _():
            sent(layer, 0)

        @pl.when(has_down)
        def _():
            sent(layer, 1)


def shards(fields, lat_taps, lon_taps, gains, w_in, w_out):
    return pl.pallas_call(
        kernel,
        out_shape=pltpu.VMEM(fields.shape, fields.dtype),
        in_specs=[pl.BlockSpec(memory_space=pl.ANY)] * 6,
        out_specs=pl.BlockSpec(memory_space=pltpu.VMEM),
        scratch_shapes=[
            pltpu.VMEM((3 * ROWS, LON + 32, C), jnp.bfloat16),
            pltpu.VMEM((3 * ROWS, LON + 32, C), jnp.bfloat16),
            pltpu.VMEM((LAYERS, ROWS, PAD + LON + 64, C), jnp.float32),
            pltpu.VMEM((TAPS, LAYERS, C), jnp.bfloat16),
            pltpu.VMEM((TAPS, LAYERS, C), jnp.bfloat16),
            pltpu.VMEM((TAPS, LAYERS, C), jnp.float32),
            pltpu.VMEM((TAPS, LAYERS, C), jnp.float32),
            pltpu.VMEM((LAYERS, C), jnp.float32),
            pltpu.VMEM((LAYERS, C, H), jnp.bfloat16),
            pltpu.VMEM((LAYERS, H, C), jnp.bfloat16),
            pltpu.VMEM((ROWS, LON, C), jnp.bfloat16),
            pltpu.VMEM((ROWS, LON, C), jnp.bfloat16),
            pltpu.SemaphoreType.DMA((LAYERS, 2)),
            pltpu.SemaphoreType.DMA((len(SENT[0]),)),
            pltpu.SemaphoreType.DMA((len(SENT[1]),)),
            pltpu.SemaphoreType.DMA((6,)),
            pltpu.SemaphoreType.REGULAR((2,)),
            pltpu.SemaphoreType.DMA((6,)),
        ],
        compiler_params=pltpu.CompilerParams(collective_id=0, has_side_effects=True),
        name="step",
    )(fields, jnp.transpose(lat_taps, (1, 0, 2)), jnp.transpose(lon_taps, (1, 0, 2)), gains, w_in, w_out)


def solution(mesh):
    return jax.shard_map(
        shards,
        mesh=mesh,
        in_specs=(P(("members", "section"), "band", None, None), P(), P(), P(), P(), P()),
        out_specs=P(("members", "section"), "band", None, None),
        check_vma=False,
    )
```

```python
import jax
import jax.numpy as jnp
from jax import lax
from jax.experimental import pallas as pl
from jax.experimental.pallas import tpu as pltpu
from jax.sharding import PartitionSpec as P

LAYERS = 2
TAPS = 9
REACH = 12
ROWS = 4
LON = 576
C = 128
H = 256
BANDS = 32
RUN = 8
RUNS = BANDS // RUN
PAD = 16
BLOCK = 48
TAIL = 512
TAIL_WIDTH = 96
MESH = pl.DeviceIdType.MESH

SENT = (
    ((0, 96), (96, 96), (192, 96), (288, 96), (384, 96), (480, 96)),
    ((16, 64), (80, 96), (176, 96), (272, 96), (368, 96), (464, 64), (528, 64)),
)
DONE = (
    ((16, 64), (80, 96), (176, 96), (272, 96), (368, 96), (464, 96)),
    ((32, 32), (64, 96), (160, 96), (256, 96), (352, 96), (448, 64)),
)
RELAYED = ((3, 4, 5), (0, 1, 2))
NEXT = ((0,), (1,), (2,), (3,), (4,), (5,))


def pointwise(mixes, lon_tap, gain, proj_in, proj_out):
    totals = []
    for mix in mixes:
        total = mix(0) * lon_tap(0)
        for k in range(1, TAPS):
            total = total + mix(3 * k) * lon_tap(k)
        totals.append(total)
    total = jnp.concatenate(totals, axis=0)
    mean = jnp.mean(total, axis=-1, keepdims=True)
    centred = total - mean
    var = jnp.mean(centred * centred, axis=-1, keepdims=True)
    normed = (centred * lax.rsqrt(var + 1e-06) * gain).astype(jnp.bfloat16)
    inner = jnp.dot(normed, proj_in, preferred_element_type=jnp.float32)
    hidden = (0.5 * inner * (1.0 + lax.erf(inner * 0.7071067811865476))).astype(jnp.bfloat16)
    return jnp.dot(hidden, proj_out, preferred_element_type=jnp.float32)


def finishing(done, mix, old, lon32, gain32, win, wout, out, last, sems):
    layer = LAYERS - 1
    copies = [pltpu.make_async_copy(done, out.at[0, :, 32:TAIL], sems.at[0])]
    copies[0].start()
    for block in range(TAIL_WIDTH // BLOCK):
        at = block * BLOCK

        def shifted(i):
            return lambda by: mix[i, 16 + at - REACH + by:16 + at - REACH + by + BLOCK, :]

        delta = pointwise(
            [shifted(i) for i in range(ROWS)], lambda k: lon32[k, layer:layer + 1, :], gain32[layer:layer + 1, :],
            win[layer], wout[layer],
        )
        for i in range(ROWS):
            value = old[i, at:at + BLOCK, :].astype(jnp.float32) + delta[i * BLOCK:(i + 1) * BLOCK]
            last[i, at:at + BLOCK, :] = value.astype(jnp.bfloat16)
        if block == 0:
            copies.append(pltpu.make_async_copy(last.at[:, 0:BLOCK], out.at[0, :, TAIL:TAIL + BLOCK], sems.at[1]))
            copies[-1].start()
    inside = LON - TAIL
    copies.append(pltpu.make_async_copy(last.at[:, BLOCK:inside], out.at[0, :, TAIL + BLOCK:LON], sems.at[2]))
    copies.append(pltpu.make_async_copy(last.at[:, inside:], out.at[0, :, 0:TAIL_WIDTH - inside], sems.at[3]))
    copies[-2].start()
    copies[-1].start()
    for started in copies:
        started.wait()


def kernel(fields, lat_taps, lon_taps, gains, w_in, w_out, done, mix, old, lon32, gain32, win, wout,
           state0, state1, mixed, lat16, lon16, lat32,
           relay0, relay1, send_sem, recv0_sem, recv1_sem, load_sem, ready_sem, relay_sem):
    band = lax.axis_index("band")
    place_in_run = lax.rem(band, RUN)
    run_index = band // RUN
    opens = place_in_run == 0
    closes = place_in_run == RUN - 1
    has_up = band > 0
    has_down = band < BANDS - 1
    inside = jnp.logical_and(has_up, has_down)
    tied_above = place_in_run >= RUN - 2
    tied_below = jnp.logical_and(place_in_run >= RUN - 3, jnp.logical_not(closes))
    states = (state0, state1)
    recv_sems = (recv0_sem, recv1_sem)
    above, below = {"band": band - 1}, {"band": band + 1}
    run_before, run_after = {"band": band - RUN}, {"band": band + RUN}
    run_start, run_end = {"band": band - (RUN - 1)}, {"band": band + (RUN - 1)}
    relays = (relay0, relay1)
    later, sooner = run_index > 0, run_index < RUNS - 1
    round_down = jnp.logical_and(closes, sooner)
    round_up = jnp.logical_and(opens, later)
    passes_down = jnp.logical_and(closes, later)
    passes_up = jnp.logical_and(opens, sooner)

    def is_relayed(layer, slot, count):
        return count >= (len(RELAYED[0]) - slot if layer == 0 else slot + 1)

    barrier = pltpu.get_barrier_semaphore()

    def greet(condition, device):
        @pl.when(condition)
        def _():
            pl.semaphore_signal(barrier, inc=1, device_id=device, device_id_type=MESH)

    greet(jnp.logical_or(place_in_run < RUN - 2, round_down), below)
    greet(jnp.logical_or(tied_above, round_up), above)
    greet(opens, run_end)
    greet(jnp.logical_or(round_down, passes_up), run_after)

    own = pltpu.make_async_copy(fields.at[0], state0.at[ROWS:2 * ROWS, 0:LON], load_sem.at[0])
    loads = [
        pltpu.make_async_copy(lat_taps, lat16, load_sem.at[1]),
        pltpu.make_async_copy(lon_taps, lon16, load_sem.at[2]),
        pltpu.make_async_copy(gains, gain32, load_sem.at[3]),
        pltpu.make_async_copy(w_in, win, load_sem.at[4]),
        pltpu.make_async_copy(w_out, wout, load_sem.at[5]),
    ]
    own.start()
    for load in loads:
        load.start()

    def copy(layer, side, piece, sending=True):
        place = states[layer]
        start, width = SENT[layer][piece]
        first = 2 * ROWS if side == 0 else 0
        source = fields.at[0, :, start:start + width] if layer == 0 else place.at[ROWS:2 * ROWS, start:start + width]
        return pltpu.make_async_remote_copy(
            src_ref=source,
            dst_ref=place.at[first:first + ROWS, start:start + width],
            send_sem=send_sem.at[layer, side],
            recv_sem=recv_sems[layer].at[piece],
            device_id=above if side == 0 else below,
            device_id_type=MESH,
        )

    def slot_of(layer, piece):
        return layer * len(RELAYED[0]) + RELAYED[layer].index(piece)

    def detour(layer, side, piece):
        start, width = SENT[layer][piece]
        source = fields.at[0, :, start:start + width] if layer == 0 else state1.at[ROWS:2 * ROWS, start:start + width]
        return pltpu.make_async_remote_copy(
            src_ref=source,
            dst_ref=relays[layer].at[:, start:start + width],
            send_sem=send_sem.at[layer, side],
            recv_sem=relay_sem.at[slot_of(layer, piece)],
            device_id=run_before if side == 0 else run_after,
            device_id_type=MESH,
        )

    def onward(layer, side, piece):
        start, width = SENT[layer][piece]
        first = 2 * ROWS if side == 0 else 0
        return pltpu.make_async_remote_copy(
            src_ref=relays[layer].at[:, start:start + width],
            dst_ref=states[layer].at[first:first + ROWS, start:start + width],
            send_sem=relay_sem.at[slot_of(layer, piece)],
            recv_sem=recv_sems[layer].at[piece],
            device_id=run_end if side == 0 else run_start,
            device_id_type=MESH,
        )

    def goes_round(layer, side, piece):
        if piece not in RELAYED[layer] or (layer == 1 and side == 0):
            return None
        slot = RELAYED[layer].index(piece)
        if side == 0:
            return jnp.logical_and(round_up, is_relayed(layer, slot, RUNS - run_index))
        return jnp.logical_and(round_down, is_relayed(layer, slot, run_index + 1))

    def send_direct(layer, side, pieces):
        for piece in pieces:
            round_about = goes_round(layer, side, piece)
            if round_about is None:
                copy(layer, side, piece).start()
            else:
                @pl.when(jnp.logical_not(round_about))
                def _():
                    copy(layer, side, piece).start()

    def send_up(layer, pieces):
        send_direct(layer, 0, pieces)

    def send_down(layer, pieces):
        send_direct(layer, 1, pieces)

    def send_round(layer, side, pieces):
        for piece in pieces:
            round_about = goes_round(layer, side, piece)
            if round_about is not None:
                @pl.when(round_about)
                def _():
                    detour(layer, side, piece).start()

    def send(layer, pieces):
        send_round(layer, 1, pieces)

        @pl.when(has_down)
        def _():
            send_down(layer, pieces)

        @pl.when(has_up)
        def _():
            send_up(layer, pieces)

    def passed(layer, side, piece):
        slot = RELAYED[layer].index(piece)
        if side == 0:
            return jnp.logical_and(passes_up, is_relayed(layer, slot, RUNS - 1 - run_index))
        return jnp.logical_and(passes_down, is_relayed(layer, slot, run_index))

    def pass_on(layer, side, piece):
        @pl.when(passed(layer, side, piece))
        def _():
            start, width = SENT[layer][piece]
            part = relays[layer].at[:, start:start + width]
            pltpu.make_async_remote_copy(
                src_ref=part, dst_ref=part, send_sem=send_sem.at[0, 0], recv_sem=relay_sem.at[slot_of(layer, piece)],
                device_id=above, device_id_type=MESH,
            ).wait_recv()
            onward(layer, side, piece).start()

    def passed_on(layer, side, piece):
        @pl.when(passed(layer, side, piece))
        def _():
            onward(layer, side, piece).wait_send()

    def awaited(layer, piece, rows):
        start, width = SENT[layer][piece]
        part = states[layer].at[0:rows, start:start + width]
        return pltpu.make_async_remote_copy(
            src_ref=part, dst_ref=part, send_sem=send_sem.at[0, 0], recv_sem=recv_sems[layer].at[piece],
            device_id=above, device_id_type=MESH,
        )

    def arrived(layer, piece):
        @pl.when(inside)
        def _():
            awaited(layer, piece, 2 * ROWS).wait_recv()

        @pl.when(jnp.logical_not(inside))
        def _():
            awaited(layer, piece, ROWS).wait_recv()

    def sent(layer, side):
        start = SENT[layer][0][0]
        part = states[layer].at[0:ROWS, start:start + LON]
        pltpu.make_async_remote_copy(
            src_ref=part, dst_ref=part, send_sem=send_sem.at[layer, side], recv_sem=recv0_sem.at[0],
            device_id=above, device_id_type=MESH,
        ).wait_send()

    all_first = range(len(SENT[0]))

    def answer(condition, which, device):
        @pl.when(condition)
        def _():
            pl.semaphore_signal(ready_sem.at[which], inc=1, device_id=device, device_id_type=MESH)

    @pl.when(jnp.logical_not(opens))
    def _():
        pl.semaphore_wait(barrier, 1 + (tied_below | round_down).astype(jnp.int32) + passes_down.astype(jnp.int32))

    @pl.when(tied_below | round_down)
    def _():
        send_down(0, all_first)

    answer(passes_down, 1, run_before)
    answer(round_down, 1, run_start)
    answer(jnp.logical_and(place_in_run > 0, place_in_run < RUN - 2), 0, above)
    answer(place_in_run == RUN - 2, 0, below)

    @pl.when(jnp.logical_not(opens | closes))
    def _():
        send_up(0, all_first)

    @pl.when(round_down)
    def _():
        pl.semaphore_wait(ready_sem.at[1], 1)
        send_round(0, 1, all_first)

    @pl.when(jnp.logical_not(tied_below))
    def _():
        pl.semaphore_wait(ready_sem.at[0], 1)

        @pl.when(closes)
        def _():
            send_up(0, all_first)

        @pl.when(jnp.logical_not(closes))
        def _():
            send_down(0, all_first)

    @pl.when(round_up)
    def _():
        pl.semaphore_wait(barrier, 2)
        send_up(0, all_first)
        send_round(0, 0, all_first)

    @pl.when(passes_up)
    def _():
        pl.semaphore_wait(ready_sem.at[1], 1)

    @pl.when(jnp.logical_not(has_up))
    def _():
        for place in states:
            place[0:ROWS] = jnp.zeros((ROWS,) + place.shape[1:], place.dtype)

    @pl.when(jnp.logical_not(has_down))
    def _():
        for place in states:
            place[2 * ROWS:] = jnp.zeros((ROWS,) + place.shape[1:], place.dtype)

    own.wait()
    for load in loads:
        load.wait()
    state0[ROWS:2 * ROWS, LON:LON + 16, :] = state0[ROWS:2 * ROWS, 0:16, :]
    lat32[...] = lat16[...].astype(jnp.float32)
    lon32[...] = lon16[...].astype(jnp.float32)

    def latmix(layer, piece):
        place = states[layer]
        start, width = SENT[layer][piece]
        for at in range(start, start + width, 16):
            rows = [place[r, at:at + 16, :].astype(jnp.float32) for r in range(3 * ROWS)]
            for i in range(ROWS):
                total = rows[i] * lat32[0, layer:layer + 1, :]
                for k in range(1, TAPS):
                    total = total + rows[i + k] * lat32[k, layer:layer + 1, :]
                total = total.astype(jnp.bfloat16).astype(jnp.float32)
                if layer == 0 or at <= TAIL:
                    mixed[layer, i, PAD + at:PAD + at + 16, :] = total
                if layer == 1 and at >= TAIL - 16:
                    mix[i, at - TAIL + 16:at - TAIL + 32, :] = total
                if at + LON < (LAYERS + 1) * 16 + LON + layer * 16 - 16:
                    if layer == 0:
                        mixed[layer, i, PAD + at + LON:PAD + at + LON + 16, :] = total
                    else:
                        mix[i, at + LON - TAIL + 16:at + LON - TAIL + 32, :] = total

    def rest(layer, start, width, store):
        def shifted(i):
            at = PAD + start - REACH
            return lambda by: mixed[layer, i, at + by:at + by + width, :]

        delta = pointwise(
            [shifted(i) for i in range(ROWS)], lambda k: lon32[k, layer:layer + 1, :], gain32[layer:layer + 1, :],
            win[layer], wout[layer],
        )
        for i in range(ROWS):
            before = states[layer][ROWS + i, start:start + width, :].astype(jnp.float32)
            store(i, start, width, (before + delta[i * width:(i + 1) * width]).astype(jnp.bfloat16))

    def keep(i, start, width, value):
        state1[ROWS + i, start:start + width, :] = value
        if start == 16:
            state1[ROWS + i, LON + 16:LON + 32, :] = value[:16]

    def finish(i, start, width, value):
        done[i, start - 32:start - 32 + width, :] = value

    def run(layer, start, width, store):
        for at in range(start, start + width, BLOCK):
            rest(layer, at, min(BLOCK, start + width - at), store)

    for piece in range(len(SENT[0])):
        if piece < 3:
            pass_on(0, 1, RELAYED[0][piece])
            pass_on(0, 0, RELAYED[0][piece])
        arrived(0, piece)
        latmix(0, piece)
        run(0, *DONE[0][piece], keep)
        if piece in (2, 3, 4):
            pass_on(1, 1, RELAYED[1][piece - 2])
        send(1, NEXT[piece])
    run(0, LON - 16, 32, keep)
    send(1, (len(SENT[1]) - 1,))

    old[...] = state1[ROWS:2 * ROWS, TAIL:TAIL + TAIL_WIDTH, :]
    for piece in range(len(SENT[1])):
        arrived(1, piece)
        latmix(1, piece)
        if piece < len(DONE[1]):
            run(1, *DONE[1][piece], finish)

    for slot in range(3):
        passed_on(0, 0, RELAYED[0][slot])
        passed_on(0, 1, RELAYED[0][slot])
        passed_on(1, 1, RELAYED[1][slot])
    for layer in range(LAYERS):
        @pl.when(has_up)
        def _():
            sent(layer, 0)

        @pl.when(has_down)
        def _():
            sent(layer, 1)


def shards(fields, lat_taps, lon_taps, gains, w_in, w_out):
    kept = (
        pltpu.VMEM((ROWS, TAIL - 32, C), jnp.bfloat16),
        pltpu.VMEM((ROWS, TAIL_WIDTH + 32, C), jnp.float32),
        pltpu.VMEM((ROWS, TAIL_WIDTH, C), jnp.bfloat16),
        pltpu.VMEM((TAPS, LAYERS, C), jnp.float32),
        pltpu.VMEM((LAYERS, C), jnp.float32),
        pltpu.VMEM((LAYERS, C, H), jnp.bfloat16),
        pltpu.VMEM((LAYERS, H, C), jnp.bfloat16),
    )
    handed = pl.pallas_call(
        kernel,
        out_shape=kept,
        in_specs=[pl.BlockSpec(memory_space=pl.ANY)] * 6,
        out_specs=[pl.BlockSpec(memory_space=pltpu.VMEM)] * len(kept),
        scratch_shapes=[
            pltpu.VMEM((3 * ROWS, LON + 32, C), jnp.bfloat16),
            pltpu.VMEM((3 * ROWS, LON + 32, C), jnp.bfloat16),
            pltpu.VMEM((LAYERS, ROWS, PAD + LON + 64, C), jnp.float32),
            pltpu.VMEM((TAPS, LAYERS, C), jnp.bfloat16),
            pltpu.VMEM((TAPS, LAYERS, C), jnp.bfloat16),
            pltpu.VMEM((TAPS, LAYERS, C), jnp.float32),
            pltpu.VMEM((ROWS, LON, C), jnp.bfloat16),
            pltpu.VMEM((ROWS, LON, C), jnp.bfloat16),
            pltpu.SemaphoreType.DMA((LAYERS, 2)),
            pltpu.SemaphoreType.DMA((len(SENT[0]),)),
            pltpu.SemaphoreType.DMA((len(SENT[1]),)),
            pltpu.SemaphoreType.DMA((6,)),
            pltpu.SemaphoreType.REGULAR((2,)),
            pltpu.SemaphoreType.DMA((6,)),
        ],
        compiler_params=pltpu.CompilerParams(collective_id=0, has_side_effects=True),
        name="step",
    )(fields, jnp.transpose(lat_taps, (1, 0, 2)), jnp.transpose(lon_taps, (1, 0, 2)), gains, w_in, w_out)
    handed = [pltpu.with_memory_space_constraint(array, pltpu.VMEM) for array in handed]
    return pl.pallas_call(
        finishing,
        out_shape=jax.ShapeDtypeStruct(fields.shape, fields.dtype),
        in_specs=[pl.BlockSpec(memory_space=pltpu.VMEM)] * len(kept),
        out_specs=pl.BlockSpec(memory_space=pl.ANY),
        scratch_shapes=[pltpu.VMEM((ROWS, TAIL_WIDTH, C), jnp.bfloat16), pltpu.SemaphoreType.DMA((4,))],
        compiler_params=pltpu.CompilerParams(vmem_limit_bytes=16 * 1024 * 1024),
        name="finishing",
    )(*handed)


def solution(mesh):
    return jax.shard_map(
        shards,
        mesh=mesh,
        in_specs=(P(("members", "section"), "band", None, None), P(), P(), P(), P(), P()),
        out_specs=P(("members", "section"), "band", None, None),
        check_vma=False,
    )
```

```python
import jax
import jax.numpy as jnp
from jax import lax
from jax.experimental import pallas as pl
from jax.experimental.pallas import tpu as pltpu
from jax.sharding import PartitionSpec as P

LAYERS = 2
TAPS = 9
REACH = 12
ROWS = 4
LON = 576
C = 128
H = 256
BANDS = 32
RUN = 8
RUNS = BANDS // RUN
PAD = 16
BLOCK = 48
TAIL = 512
TAIL_WIDTH = 96
MESH = pl.DeviceIdType.MESH

SENT = (
    ((0, 96), (96, 96), (192, 96), (288, 96), (384, 96), (480, 96)),
    ((16, 64), (80, 96), (176, 96), (272, 96), (368, 96), (464, 64), (528, 64)),
)
DONE = (
    ((16, 64), (80, 96), (176, 96), (272, 96), (368, 96), (464, 96)),
    ((32, 32), (64, 96), (160, 96), (256, 96), (352, 96), (448, 64)),
)
RELAYED = ((3, 4, 5), (0, 1, 2))
NEXT = ((0,), (1,), (2,), (3,), (4,), (5,))


def pointwise(mixes, lon_tap, gain, proj_in, proj_out):
    totals = []
    for mix in mixes:
        total = mix(0) * lon_tap(0)
        for k in range(1, TAPS):
            total = total + mix(3 * k) * lon_tap(k)
        totals.append(total)
    total = jnp.concatenate(totals, axis=0)
    mean = jnp.mean(total, axis=-1, keepdims=True)
    centred = total - mean
    var = jnp.mean(centred * centred, axis=-1, keepdims=True)
    normed = (centred * lax.rsqrt(var + 1e-06) * gain).astype(jnp.bfloat16)
    inner = jnp.dot(normed, proj_in, preferred_element_type=jnp.float32)
    hidden = (0.5 * inner * (1.0 + lax.erf(inner * 0.7071067811865476))).astype(jnp.bfloat16)
    return jnp.dot(hidden, proj_out, preferred_element_type=jnp.float32)


def finishing(done, mix, old, lon32, gain32, win, wout, out, last, sems):
    layer = LAYERS - 1
    copies = [pltpu.make_async_copy(done, out.at[0, :, 32:TAIL], sems.at[0])]
    copies[0].start()
    for block in range(TAIL_WIDTH // BLOCK):
        at = block * BLOCK

        def shifted(i):
            return lambda by: mix[i, 16 + at - REACH + by:16 + at - REACH + by + BLOCK, :]

        delta = pointwise(
            [shifted(i) for i in range(ROWS)], lambda k: lon32[k, layer:layer + 1, :], gain32[layer:layer + 1, :],
            win[layer], wout[layer],
        )
        for i in range(ROWS):
            value = old[i, at:at + BLOCK, :].astype(jnp.float32) + delta[i * BLOCK:(i + 1) * BLOCK]
            last[i, at:at + BLOCK, :] = value.astype(jnp.bfloat16)
        if block == 0:
            copies.append(pltpu.make_async_copy(last.at[:, 0:BLOCK], out.at[0, :, TAIL:TAIL + BLOCK], sems.at[1]))
            copies[-1].start()
    inside = LON - TAIL
    copies.append(pltpu.make_async_copy(last.at[:, BLOCK:inside], out.at[0, :, TAIL + BLOCK:LON], sems.at[2]))
    copies.append(pltpu.make_async_copy(last.at[:, inside:], out.at[0, :, 0:TAIL_WIDTH - inside], sems.at[3]))
    copies[-2].start()
    copies[-1].start()
    for started in copies:
        started.wait()


def kernel(fields, lat_taps, lon_taps, gains, w_in, w_out, done, mix, old, lon32, gain32, win, wout,
           state0, state1, mixed, lat16, lon16, lat32,
           relay0, relay1, send_sem, recv0_sem, recv1_sem, load_sem, ready_sem, relay_sem):
    band = lax.axis_index("band")
    place_in_run = lax.rem(band, RUN)
    run_index = band // RUN
    opens = place_in_run == 0
    closes = place_in_run == RUN - 1
    has_up = band > 0
    has_down = band < BANDS - 1
    inside = jnp.logical_and(has_up, has_down)
    tied_above = place_in_run >= RUN - 2
    tied_below = jnp.logical_and(place_in_run >= RUN - 3, jnp.logical_not(closes))
    states = (state0, state1)
    recv_sems = (recv0_sem, recv1_sem)
    above, below = {"band": band - 1}, {"band": band + 1}
    run_before, run_after = {"band": band - RUN}, {"band": band + RUN}
    run_start, run_end = {"band": band - (RUN - 1)}, {"band": band + (RUN - 1)}
    relays = (relay0, relay1)
    later, sooner = run_index > 0, run_index < RUNS - 1
    round_down = jnp.logical_and(closes, sooner)
    round_up = jnp.logical_and(opens, later)
    passes_down = jnp.logical_and(closes, later)
    passes_up = jnp.logical_and(opens, sooner)

    def is_relayed(layer, slot, count):
        return count >= (len(RELAYED[0]) - slot if layer == 0 else slot + 1)

    barrier = pltpu.get_barrier_semaphore()

    def greet(condition, device):
        @pl.when(condition)
        def _():
            pl.semaphore_signal(barrier, inc=1, device_id=device, device_id_type=MESH)

    greet(jnp.logical_or(place_in_run < RUN - 2, round_down), below)
    greet(jnp.logical_or(tied_above, round_up), above)
    greet(opens, run_end)
    greet(jnp.logical_or(round_down, passes_up), run_after)

    own = pltpu.make_async_copy(fields.at[0], state0.at[ROWS:2 * ROWS, 0:LON], load_sem.at[0])
    loads = [
        pltpu.make_async_copy(lat_taps, lat16, load_sem.at[1]),
        pltpu.make_async_copy(lon_taps, lon16, load_sem.at[2]),
        pltpu.make_async_copy(gains, gain32, load_sem.at[3]),
        pltpu.make_async_copy(w_in, win, load_sem.at[4]),
        pltpu.make_async_copy(w_out, wout, load_sem.at[5]),
    ]
    own.start()
    for load in loads:
        load.start()

    def copy(layer, side, piece, sending=True):
        place = states[layer]
        start, width = SENT[layer][piece]
        first = 2 * ROWS if side == 0 else 0
        source = fields.at[0, :, start:start + width] if layer == 0 else place.at[ROWS:2 * ROWS, start:start + width]
        return pltpu.make_async_remote_copy(
            src_ref=source,
            dst_ref=place.at[first:first + ROWS, start:start + width],
            send_sem=send_sem.at[layer, side],
            recv_sem=recv_sems[layer].at[piece],
            device_id=above if side == 0 else below,
            device_id_type=MESH,
        )

    def slot_of(layer, piece):
        return layer * len(RELAYED[0]) + RELAYED[layer].index(piece)

    def detour(layer, side, piece):
        start, width = SENT[layer][piece]
        source = fields.at[0, :, start:start + width] if layer == 0 else state1.at[ROWS:2 * ROWS, start:start + width]
        return pltpu.make_async_remote_copy(
            src_ref=source,
            dst_ref=relays[layer].at[:, start:start + width],
            send_sem=send_sem.at[layer, side],
            recv_sem=relay_sem.at[slot_of(layer, piece)],
            device_id=run_before if side == 0 else run_after,
            device_id_type=MESH,
        )

    def onward(layer, side, piece):
        start, width = SENT[layer][piece]
        first = 2 * ROWS if side == 0 else 0
        return pltpu.make_async_remote_copy(
            src_ref=relays[layer].at[:, start:start + width],
            dst_ref=states[layer].at[first:first + ROWS, start:start + width],
            send_sem=relay_sem.at[slot_of(layer, piece)],
            recv_sem=recv_sems[layer].at[piece],
            device_id=run_end if side == 0 else run_start,
            device_id_type=MESH,
        )

    def goes_round(layer, side, piece):
        if piece not in RELAYED[layer] or (layer == 1 and side == 0):
            return None
        slot = RELAYED[layer].index(piece)
        if side == 0:
            return jnp.logical_and(round_up, is_relayed(layer, slot, RUNS - run_index))
        return jnp.logical_and(round_down, is_relayed(layer, slot, run_index + 1))

    def send_direct(layer, side, pieces):
        for piece in pieces:
            round_about = goes_round(layer, side, piece)
            if round_about is None:
                copy(layer, side, piece).start()
            else:
                @pl.when(jnp.logical_not(round_about))
                def _():
                    copy(layer, side, piece).start()

    def send_up(layer, pieces):
        send_direct(layer, 0, pieces)

    def send_down(layer, pieces):
        send_direct(layer, 1, pieces)

    def send_round(layer, side, pieces):
        for piece in pieces:
            round_about = goes_round(layer, side, piece)
            if round_about is not None:
                @pl.when(round_about)
                def _():
                    detour(layer, side, piece).start()

    def send(layer, pieces):
        send_round(layer, 1, pieces)

        @pl.when(has_down)
        def _():
            send_down(layer, pieces)

        @pl.when(has_up)
        def _():
            send_up(layer, pieces)

    def passed(layer, side, piece):
        slot = RELAYED[layer].index(piece)
        if side == 0:
            return jnp.logical_and(passes_up, is_relayed(layer, slot, RUNS - 1 - run_index))
        return jnp.logical_and(passes_down, is_relayed(layer, slot, run_index))

    def pass_on(layer, side, piece, counts=(1, 2, 3)):
        count = RUNS - 1 - run_index if side == 0 else run_index
        now = passed(layer, side, piece)
        for other in (1, 2, 3):
            if other not in counts:
                now = jnp.logical_and(now, count != other)

        @pl.when(now)
        def _():
            start, width = SENT[layer][piece]
            part = relays[layer].at[:, start:start + width]
            pltpu.make_async_remote_copy(
                src_ref=part, dst_ref=part, send_sem=send_sem.at[0, 0], recv_sem=relay_sem.at[slot_of(layer, piece)],
                device_id=above, device_id_type=MESH,
            ).wait_recv()
            onward(layer, side, piece).start()

    def passed_on(layer, side, piece):
        @pl.when(passed(layer, side, piece))
        def _():
            onward(layer, side, piece).wait_send()

    def awaited(layer, piece, rows):
        start, width = SENT[layer][piece]
        part = states[layer].at[0:rows, start:start + width]
        return pltpu.make_async_remote_copy(
            src_ref=part, dst_ref=part, send_sem=send_sem.at[0, 0], recv_sem=recv_sems[layer].at[piece],
            device_id=above, device_id_type=MESH,
        )

    def arrived(layer, piece):
        @pl.when(inside)
        def _():
            awaited(layer, piece, 2 * ROWS).wait_recv()

        @pl.when(jnp.logical_not(inside))
        def _():
            awaited(layer, piece, ROWS).wait_recv()

    def sent(layer, side):
        start = SENT[layer][0][0]
        part = states[layer].at[0:ROWS, start:start + LON]
        pltpu.make_async_remote_copy(
            src_ref=part, dst_ref=part, send_sem=send_sem.at[layer, side], recv_sem=recv0_sem.at[0],
            device_id=above, device_id_type=MESH,
        ).wait_send()

    all_first = range(len(SENT[0]))

    def answer(condition, which, device):
        @pl.when(condition)
        def _():
            pl.semaphore_signal(ready_sem.at[which], inc=1, device_id=device, device_id_type=MESH)

    @pl.when(jnp.logical_not(opens))
    def _():
        pl.semaphore_wait(barrier, 1 + (tied_below | round_down).astype(jnp.int32) + passes_down.astype(jnp.int32))

    @pl.when(tied_below | round_down)
    def _():
        send_down(0, all_first)

    answer(passes_down, 1, run_before)
    answer(round_down, 1, run_start)
    answer(jnp.logical_and(place_in_run > 0, place_in_run < RUN - 2), 0, above)
    answer(place_in_run == RUN - 2, 0, below)

    @pl.when(jnp.logical_not(opens | closes))
    def _():
        send_up(0, all_first)

    @pl.when(round_down)
    def _():
        pl.semaphore_wait(ready_sem.at[1], 1)
        send_round(0, 1, all_first)

    @pl.when(jnp.logical_not(tied_below))
    def _():
        pl.semaphore_wait(ready_sem.at[0], 1)

        @pl.when(closes)
        def _():
            send_up(0, all_first)

        @pl.when(jnp.logical_not(closes))
        def _():
            send_down(0, all_first)

    @pl.when(round_up)
    def _():
        pl.semaphore_wait(barrier, 2)
        send_up(0, all_first)
        send_round(0, 0, all_first)

    @pl.when(passes_up)
    def _():
        pl.semaphore_wait(ready_sem.at[1], 1)

    @pl.when(jnp.logical_not(has_up))
    def _():
        for place in states:
            place[0:ROWS] = jnp.zeros((ROWS,) + place.shape[1:], place.dtype)

    @pl.when(jnp.logical_not(has_down))
    def _():
        for place in states:
            place[2 * ROWS:] = jnp.zeros((ROWS,) + place.shape[1:], place.dtype)

    own.wait()
    for load in loads:
        load.wait()
    state0[ROWS:2 * ROWS, LON:LON + 16, :] = state0[ROWS:2 * ROWS, 0:16, :]
    lat32[...] = lat16[...].astype(jnp.float32)
    lon32[...] = lon16[...].astype(jnp.float32)

    def latmix(layer, piece):
        place = states[layer]
        start, width = SENT[layer][piece]
        for at in range(start, start + width, 16):
            rows = [place[r, at:at + 16, :].astype(jnp.float32) for r in range(3 * ROWS)]
            for i in range(ROWS):
                total = rows[i] * lat32[0, layer:layer + 1, :]
                for k in range(1, TAPS):
                    total = total + rows[i + k] * lat32[k, layer:layer + 1, :]
                total = total.astype(jnp.bfloat16).astype(jnp.float32)
                if layer == 0 or at <= TAIL:
                    mixed[layer, i, PAD + at:PAD + at + 16, :] = total
                if layer == 1 and at >= TAIL - 16:
                    mix[i, at - TAIL + 16:at - TAIL + 32, :] = total
                if at + LON < (LAYERS + 1) * 16 + LON + layer * 16 - 16:
                    if layer == 0:
                        mixed[layer, i, PAD + at + LON:PAD + at + LON + 16, :] = total
                    else:
                        mix[i, at + LON - TAIL + 16:at + LON - TAIL + 32, :] = total

    def rest(layer, start, width, store):
        def shifted(i):
            at = PAD + start - REACH
            return lambda by: mixed[layer, i, at + by:at + by + width, :]

        delta = pointwise(
            [shifted(i) for i in range(ROWS)], lambda k: lon32[k, layer:layer + 1, :], gain32[layer:layer + 1, :],
            win[layer], wout[layer],
        )
        for i in range(ROWS):
            before = states[layer][ROWS + i, start:start + width, :].astype(jnp.float32)
            store(i, start, width, (before + delta[i * width:(i + 1) * width]).astype(jnp.bfloat16))

    def keep(i, start, width, value):
        state1[ROWS + i, start:start + width, :] = value
        if start == 16:
            state1[ROWS + i, LON + 16:LON + 32, :] = value[:16]

    def finish(i, start, width, value):
        done[i, start - 32:start - 32 + width, :] = value

    def run(layer, start, width, store):
        for at in range(start, start + width, BLOCK):
            rest(layer, at, min(BLOCK, start + width - at), store)

    for piece in range(len(SENT[0])):
        for relayed, counts in (((3, (3,)), (4, (2,)), (5, (1,))), ((4, (3,)), (5, (2,))), ((5, (3,)),))[piece] if piece < 3 else ():
            pass_on(0, 1, relayed, counts)
        for relayed, counts in (((3, (3,)),), ((4, (2, 3)), (5, (1,))), ((5, (2, 3)),))[piece] if piece < 3 else ():
            pass_on(0, 0, relayed, counts)
        arrived(0, piece)
        latmix(0, piece)
        run(0, *DONE[0][piece], keep)
        if piece in (2, 3, 4):
            pass_on(1, 1, RELAYED[1][piece - 2])
        send(1, NEXT[piece])
    run(0, LON - 16, 32, keep)
    send(1, (len(SENT[1]) - 1,))

    old[...] = state1[ROWS:2 * ROWS, TAIL:TAIL + TAIL_WIDTH, :]
    for piece in range(len(SENT[1])):
        arrived(1, piece)
        latmix(1, piece)
        if piece < len(DONE[1]):
            run(1, *DONE[1][piece], finish)

    for slot in range(3):
        passed_on(0, 0, RELAYED[0][slot])
        passed_on(0, 1, RELAYED[0][slot])
        passed_on(1, 1, RELAYED[1][slot])
    for layer in range(LAYERS):
        @pl.when(has_up)
        def _():
            sent(layer, 0)

        @pl.when(has_down)
        def _():
            sent(layer, 1)


def shards(fields, lat_taps, lon_taps, gains, w_in, w_out):
    kept = (
        pltpu.VMEM((ROWS, TAIL - 32, C), jnp.bfloat16),
        pltpu.VMEM((ROWS, TAIL_WIDTH + 32, C), jnp.float32),
        pltpu.VMEM((ROWS, TAIL_WIDTH, C), jnp.bfloat16),
        pltpu.VMEM((TAPS, LAYERS, C), jnp.float32),
        pltpu.VMEM((LAYERS, C), jnp.float32),
        pltpu.VMEM((LAYERS, C, H), jnp.bfloat16),
        pltpu.VMEM((LAYERS, H, C), jnp.bfloat16),
    )
    handed = pl.pallas_call(
        kernel,
        out_shape=kept,
        in_specs=[pl.BlockSpec(memory_space=pl.ANY)] * 6,
        out_specs=[pl.BlockSpec(memory_space=pltpu.VMEM)] * len(kept),
        scratch_shapes=[
            pltpu.VMEM((3 * ROWS, LON + 32, C), jnp.bfloat16),
            pltpu.VMEM((3 * ROWS, LON + 32, C), jnp.bfloat16),
            pltpu.VMEM((LAYERS, ROWS, PAD + LON + 64, C), jnp.float32),
            pltpu.VMEM((TAPS, LAYERS, C), jnp.bfloat16),
            pltpu.VMEM((TAPS, LAYERS, C), jnp.bfloat16),
            pltpu.VMEM((TAPS, LAYERS, C), jnp.float32),
            pltpu.VMEM((ROWS, LON, C), jnp.bfloat16),
            pltpu.VMEM((ROWS, LON, C), jnp.bfloat16),
            pltpu.SemaphoreType.DMA((LAYERS, 2)),
            pltpu.SemaphoreType.DMA((len(SENT[0]),)),
            pltpu.SemaphoreType.DMA((len(SENT[1]),)),
            pltpu.SemaphoreType.DMA((6,)),
            pltpu.SemaphoreType.REGULAR((2,)),
            pltpu.SemaphoreType.DMA((6,)),
        ],
        compiler_params=pltpu.CompilerParams(collective_id=0, has_side_effects=True),
        name="step",
    )(fields, jnp.transpose(lat_taps, (1, 0, 2)), jnp.transpose(lon_taps, (1, 0, 2)), gains, w_in, w_out)
    handed = [pltpu.with_memory_space_constraint(array, pltpu.VMEM) for array in handed]
    return pl.pallas_call(
        finishing,
        out_shape=jax.ShapeDtypeStruct(fields.shape, fields.dtype),
        in_specs=[pl.BlockSpec(memory_space=pltpu.VMEM)] * len(kept),
        out_specs=pl.BlockSpec(memory_space=pl.ANY),
        scratch_shapes=[pltpu.VMEM((ROWS, TAIL_WIDTH, C), jnp.bfloat16), pltpu.SemaphoreType.DMA((4,))],
        compiler_params=pltpu.CompilerParams(vmem_limit_bytes=16 * 1024 * 1024),
        name="finishing",
    )(*handed)


def solution(mesh):
    return jax.shard_map(
        shards,
        mesh=mesh,
        in_specs=(P(("members", "section"), "band", None, None), P(), P(), P(), P(), P()),
        out_specs=P(("members", "section"), "band", None, None),
        check_vma=False,
    )
```

```python
import jax
import jax.numpy as jnp
from jax import lax
from jax.experimental import pallas as pl
from jax.experimental.pallas import tpu as pltpu
from jax.sharding import PartitionSpec as P

LAYERS = 2
TAPS = 9
REACH = 12
ROWS = 4
LON = 576
C = 128
H = 256
BANDS = 32
RUN = 8
RUNS = BANDS // RUN
PAD = 16
BLOCK = 48
TAIL = 512
TAIL_WIDTH = 96
MESH = pl.DeviceIdType.MESH

SENT = (
    ((0, 96), (96, 96), (192, 96), (288, 96), (384, 96), (480, 96)),
    ((16, 64), (80, 96), (176, 96), (272, 96), (368, 96), (464, 64), (528, 64)),
)
DONE = (
    ((16, 64), (80, 96), (176, 96), (272, 96), (368, 96), (464, 96)),
    ((32, 32), (64, 96), (160, 96), (256, 96), (352, 96), (448, 64)),
)
RELAYED = ((3, 4, 5), (0, 1, 2))
NEXT = ((0,), (1,), (2,), (3,), (4,), (5,))


def pointwise(mixes, lon_tap, gain, proj_in, proj_out):
    totals = []
    for mix in mixes:
        total = mix(0) * lon_tap(0)
        for k in range(1, TAPS):
            total = total + mix(3 * k) * lon_tap(k)
        totals.append(total)
    total = jnp.concatenate(totals, axis=0)
    mean = jnp.mean(total, axis=-1, keepdims=True)
    centred = total - mean
    var = jnp.mean(centred * centred, axis=-1, keepdims=True)
    normed = (centred * lax.rsqrt(var + 1e-06) * gain).astype(jnp.bfloat16)
    inner = jnp.dot(normed, proj_in, preferred_element_type=jnp.float32)
    hidden = (0.5 * inner * (1.0 + lax.erf(inner * 0.7071067811865476))).astype(jnp.bfloat16)
    return jnp.dot(hidden, proj_out, preferred_element_type=jnp.float32)


def finishing(done, mix, old, lon32, gain32, win, wout, out, last, sems):
    layer = LAYERS - 1
    copies = [pltpu.make_async_copy(done, out.at[0, :, 32:TAIL], sems.at[0])]
    copies[0].start()
    for block in range(TAIL_WIDTH // BLOCK):
        at = block * BLOCK

        def shifted(i):
            return lambda by: mix[i, 16 + at - REACH + by:16 + at - REACH + by + BLOCK, :]

        delta = pointwise(
            [shifted(i) for i in range(ROWS)], lambda k: lon32[k, layer:layer + 1, :], gain32[layer:layer + 1, :],
            win[layer], wout[layer],
        )
        for i in range(ROWS):
            value = old[i, at:at + BLOCK, :].astype(jnp.float32) + delta[i * BLOCK:(i + 1) * BLOCK]
            last[i, at:at + BLOCK, :] = value.astype(jnp.bfloat16)
        if block == 0:
            copies.append(pltpu.make_async_copy(last.at[:, 0:BLOCK], out.at[0, :, TAIL:TAIL + BLOCK], sems.at[1]))
            copies[-1].start()
    inside = LON - TAIL
    copies.append(pltpu.make_async_copy(last.at[:, BLOCK:inside], out.at[0, :, TAIL + BLOCK:LON], sems.at[2]))
    copies.append(pltpu.make_async_copy(last.at[:, inside:], out.at[0, :, 0:TAIL_WIDTH - inside], sems.at[3]))
    copies[-2].start()
    copies[-1].start()
    for started in copies:
        started.wait()


def kernel(fields, lat_taps, lon_taps, gains, w_in, w_out, done, mix, old, lon32, gain32, win, wout,
           state0, state1, mixed, taps16, lat32,
           relay0, relay1, send_sem, recv0_sem, recv1_sem, load_sem, ready_sem, relay_sem):
    band = lax.axis_index("band")
    place_in_run = lax.rem(band, RUN)
    run_index = band // RUN
    opens = place_in_run == 0
    closes = place_in_run == RUN - 1
    has_up = band > 0
    has_down = band < BANDS - 1
    inside = jnp.logical_and(has_up, has_down)
    tied_above = place_in_run >= RUN - 2
    tied_below = jnp.logical_and(place_in_run >= RUN - 3, jnp.logical_not(closes))
    states = (state0, state1)
    recv_sems = (recv0_sem, recv1_sem)
    above, below = {"band": band - 1}, {"band": band + 1}
    run_before, run_after = {"band": band - RUN}, {"band": band + RUN}
    run_start, run_end = {"band": band - (RUN - 1)}, {"band": band + (RUN - 1)}
    relays = (relay0, relay1)
    later, sooner = run_index > 0, run_index < RUNS - 1
    round_down = jnp.logical_and(closes, sooner)
    round_up = jnp.logical_and(opens, later)
    passes_down = jnp.logical_and(closes, later)
    passes_up = jnp.logical_and(opens, sooner)

    def is_relayed(layer, slot, count):
        return count >= (len(RELAYED[0]) - slot if layer == 0 else slot + 1)

    barrier = pltpu.get_barrier_semaphore()

    def greet(condition, device):
        @pl.when(condition)
        def _():
            pl.semaphore_signal(barrier, inc=1, device_id=device, device_id_type=MESH)

    greet(jnp.logical_or(place_in_run < RUN - 2, round_down), below)
    greet(jnp.logical_or(tied_above, round_up), above)
    greet(opens, run_end)
    greet(jnp.logical_or(round_down, passes_up), run_after)

    own = pltpu.make_async_copy(fields.at[0], state0.at[ROWS:2 * ROWS, 0:LON], load_sem.at[0])
    loads = [
        pltpu.make_async_copy(lat_taps, taps16.at[0], load_sem.at[1]),
        pltpu.make_async_copy(lon_taps, taps16.at[1], load_sem.at[1]),
        pltpu.make_async_copy(gains, gain32, load_sem.at[2]),
        pltpu.make_async_copy(w_in, win, load_sem.at[3]),
        pltpu.make_async_copy(w_out, wout, load_sem.at[4]),
    ]
    own.start()
    for load in loads:
        load.start()

    def copy(layer, side, piece, sending=True):
        place = states[layer]
        start, width = SENT[layer][piece]
        first = 2 * ROWS if side == 0 else 0
        source = fields.at[0, :, start:start + width] if layer == 0 else place.at[ROWS:2 * ROWS, start:start + width]
        return pltpu.make_async_remote_copy(
            src_ref=source,
            dst_ref=place.at[first:first + ROWS, start:start + width],
            send_sem=send_sem.at[layer, side],
            recv_sem=recv_sems[layer].at[piece],
            device_id=above if side == 0 else below,
            device_id_type=MESH,
        )

    def slot_of(layer, piece):
        return layer * len(RELAYED[0]) + RELAYED[layer].index(piece)

    def detour(layer, side, piece):
        start, width = SENT[layer][piece]
        source = fields.at[0, :, start:start + width] if layer == 0 else state1.at[ROWS:2 * ROWS, start:start + width]
        return pltpu.make_async_remote_copy(
            src_ref=source,
            dst_ref=relays[layer].at[:, start:start + width],
            send_sem=send_sem.at[layer, side],
            recv_sem=relay_sem.at[slot_of(layer, piece)],
            device_id=run_before if side == 0 else run_after,
            device_id_type=MESH,
        )

    def onward(layer, side, piece):
        start, width = SENT[layer][piece]
        first = 2 * ROWS if side == 0 else 0
        return pltpu.make_async_remote_copy(
            src_ref=relays[layer].at[:, start:start + width],
            dst_ref=states[layer].at[first:first + ROWS, start:start + width],
            send_sem=relay_sem.at[slot_of(layer, piece)],
            recv_sem=recv_sems[layer].at[piece],
            device_id=run_end if side == 0 else run_start,
            device_id_type=MESH,
        )

    def goes_round(layer, side, piece):
        if piece not in RELAYED[layer] or (layer == 1 and side == 0):
            return None
        slot = RELAYED[layer].index(piece)
        if side == 0:
            return jnp.logical_and(round_up, is_relayed(layer, slot, RUNS - run_index))
        return jnp.logical_and(round_down, is_relayed(layer, slot, run_index + 1))

    def send_direct(layer, side, pieces):
        for piece in pieces:
            round_about = goes_round(layer, side, piece)
            if round_about is None:
                copy(layer, side, piece).start()
            else:
                @pl.when(jnp.logical_not(round_about))
                def _():
                    copy(layer, side, piece).start()

    def send_up(layer, pieces):
        send_direct(layer, 0, pieces)

    def send_down(layer, pieces):
        send_direct(layer, 1, pieces)

    def send_round(layer, side, pieces):
        for piece in pieces:
            round_about = goes_round(layer, side, piece)
            if round_about is not None:
                @pl.when(round_about)
                def _():
                    detour(layer, side, piece).start()

    def send(layer, pieces):
        send_round(layer, 1, pieces)

        @pl.when(has_down)
        def _():
            send_down(layer, pieces)

        @pl.when(has_up)
        def _():
            send_up(layer, pieces)

    def passed(layer, side, piece):
        slot = RELAYED[layer].index(piece)
        if side == 0:
            return jnp.logical_and(passes_up, is_relayed(layer, slot, RUNS - 1 - run_index))
        return jnp.logical_and(passes_down, is_relayed(layer, slot, run_index))

    def pass_on(layer, side, piece, counts=(1, 2, 3)):
        count = RUNS - 1 - run_index if side == 0 else run_index
        now = passed(layer, side, piece)
        for other in (1, 2, 3):
            if other not in counts:
                now = jnp.logical_and(now, count != other)

        @pl.when(now)
        def _():
            start, width = SENT[layer][piece]
            part = relays[layer].at[:, start:start + width]
            pltpu.make_async_remote_copy(
                src_ref=part, dst_ref=part, send_sem=send_sem.at[0, 0], recv_sem=relay_sem.at[slot_of(layer, piece)],
                device_id=above, device_id_type=MESH,
            ).wait_recv()
            onward(layer, side, piece).start()

    def passed_on(layer, side, piece):
        @pl.when(passed(layer, side, piece))
        def _():
            onward(layer, side, piece).wait_send()

    def awaited(layer, piece, rows):
        start, width = SENT[layer][piece]
        part = states[layer].at[0:rows, start:start + width]
        return pltpu.make_async_remote_copy(
            src_ref=part, dst_ref=part, send_sem=send_sem.at[0, 0], recv_sem=recv_sems[layer].at[piece],
            device_id=above, device_id_type=MESH,
        )

    def arrived(layer, piece):
        @pl.when(inside)
        def _():
            awaited(layer, piece, 2 * ROWS).wait_recv()

        @pl.when(jnp.logical_not(inside))
        def _():
            awaited(layer, piece, ROWS).wait_recv()

    def sent(layer, side):
        start = SENT[layer][0][0]
        part = states[layer].at[0:ROWS, start:start + LON]
        pltpu.make_async_remote_copy(
            src_ref=part, dst_ref=part, send_sem=send_sem.at[layer, side], recv_sem=recv0_sem.at[0],
            device_id=above, device_id_type=MESH,
        ).wait_send()

    all_first = range(len(SENT[0]))

    def answer(condition, which, device):
        @pl.when(condition)
        def _():
            pl.semaphore_signal(ready_sem.at[which], inc=1, device_id=device, device_id_type=MESH)

    @pl.when(jnp.logical_not(opens))
    def _():
        pl.semaphore_wait(barrier, 1 + (tied_below | round_down).astype(jnp.int32) + passes_down.astype(jnp.int32))

    @pl.when(tied_below | round_down)
    def _():
        send_down(0, all_first)

    answer(passes_down, 1, run_before)
    answer(round_down, 1, run_start)
    answer(jnp.logical_and(place_in_run > 0, place_in_run < RUN - 2), 0, above)
    answer(place_in_run == RUN - 2, 0, below)

    @pl.when(jnp.logical_not(opens | closes))
    def _():
        send_up(0, all_first)

    @pl.when(round_down)
    def _():
        pl.semaphore_wait(ready_sem.at[1], 1)
        send_round(0, 1, all_first)

    @pl.when(jnp.logical_not(tied_below))
    def _():
        pl.semaphore_wait(ready_sem.at[0], 1)

        @pl.when(closes)
        def _():
            send_up(0, all_first)

        @pl.when(jnp.logical_not(closes))
        def _():
            send_down(0, all_first)

    @pl.when(round_up)
    def _():
        pl.semaphore_wait(barrier, 2)
        send_up(0, all_first)
        send_round(0, 0, all_first)

    @pl.when(passes_up)
    def _():
        pl.semaphore_wait(ready_sem.at[1], 1)

    @pl.when(jnp.logical_not(has_up))
    def _():
        for place in states:
            place[0:ROWS] = jnp.zeros((ROWS,) + place.shape[1:], place.dtype)

    @pl.when(jnp.logical_not(has_down))
    def _():
        for place in states:
            place[2 * ROWS:] = jnp.zeros((ROWS,) + place.shape[1:], place.dtype)

    own.wait()
    pltpu.make_async_copy(taps16, taps16, load_sem.at[1]).wait()
    for load in loads[2:]:
        load.wait()
    state0[ROWS:2 * ROWS, LON:LON + 16, :] = state0[ROWS:2 * ROWS, 0:16, :]
    lat32[...] = taps16[0].astype(jnp.float32)
    lon32[...] = taps16[1].astype(jnp.float32)

    def latmix(layer, piece):
        place = states[layer]
        start, width = SENT[layer][piece]
        for at in range(start, start + width, 16):
            rows = [place[r, at:at + 16, :].astype(jnp.float32) for r in range(3 * ROWS)]
            for i in range(ROWS):
                total = rows[i] * lat32[0, layer:layer + 1, :]
                for k in range(1, TAPS):
                    total = total + rows[i + k] * lat32[k, layer:layer + 1, :]
                total = total.astype(jnp.bfloat16).astype(jnp.float32)
                if layer == 0 or at <= TAIL:
                    mixed[layer, i, PAD + at:PAD + at + 16, :] = total
                if layer == 1 and at >= TAIL - 16:
                    mix[i, at - TAIL + 16:at - TAIL + 32, :] = total
                if at + LON < (LAYERS + 1) * 16 + LON + layer * 16 - 16:
                    if layer == 0:
                        mixed[layer, i, PAD + at + LON:PAD + at + LON + 16, :] = total
                    else:
                        mix[i, at + LON - TAIL + 16:at + LON - TAIL + 32, :] = total

    def rest(layer, start, width, store):
        def shifted(i):
            at = PAD + start - REACH
            return lambda by: mixed[layer, i, at + by:at + by + width, :]

        delta = pointwise(
            [shifted(i) for i in range(ROWS)], lambda k: lon32[k, layer:layer + 1, :], gain32[layer:layer + 1, :],
            win[layer], wout[layer],
        )
        for i in range(ROWS):
            before = states[layer][ROWS + i, start:start + width, :].astype(jnp.float32)
            store(i, start, width, (before + delta[i * width:(i + 1) * width]).astype(jnp.bfloat16))

    def keep(i, start, width, value):
        state1[ROWS + i, start:start + width, :] = value
        if start == 16:
            state1[ROWS + i, LON + 16:LON + 32, :] = value[:16]

    def finish(i, start, width, value):
        done[i, start - 32:start - 32 + width, :] = value

    def run(layer, start, width, store):
        for at in range(start, start + width, BLOCK):
            rest(layer, at, min(BLOCK, start + width - at), store)

    for piece in range(len(SENT[0])):
        for relayed, counts in (((3, (3,)), (4, (2,)), (5, (1,))), ((4, (3,)), (5, (2,))), ((5, (3,)),))[piece] if piece < 3 else ():
            pass_on(0, 1, relayed, counts)
        for relayed, counts in (((3, (3,)),), ((4, (2, 3)), (5, (1,))), ((5, (2, 3)),))[piece] if piece < 3 else ():
            pass_on(0, 0, relayed, counts)
        arrived(0, piece)
        latmix(0, piece)
        run(0, *DONE[0][piece], keep)
        if piece in (2, 3, 4):
            pass_on(1, 1, RELAYED[1][piece - 2])
        send(1, NEXT[piece])
    run(0, LON - 16, 32, keep)
    send(1, (len(SENT[1]) - 1,))

    old[...] = state1[ROWS:2 * ROWS, TAIL:TAIL + TAIL_WIDTH, :]
    for piece in range(len(SENT[1])):
        arrived(1, piece)
        latmix(1, piece)
        if piece < len(DONE[1]):
            run(1, *DONE[1][piece], finish)

    for slot in range(3):
        passed_on(0, 0, RELAYED[0][slot])
        passed_on(0, 1, RELAYED[0][slot])
        passed_on(1, 1, RELAYED[1][slot])
    for layer in range(LAYERS):
        @pl.when(has_up)
        def _():
            sent(layer, 0)

        @pl.when(has_down)
        def _():
            sent(layer, 1)


def shards(fields, lat_taps, lon_taps, gains, w_in, w_out):
    kept = (
        pltpu.VMEM((ROWS, TAIL - 32, C), jnp.bfloat16),
        pltpu.VMEM((ROWS, TAIL_WIDTH + 32, C), jnp.float32),
        pltpu.VMEM((ROWS, TAIL_WIDTH, C), jnp.bfloat16),
        pltpu.VMEM((TAPS, LAYERS, C), jnp.float32),
        pltpu.VMEM((LAYERS, C), jnp.float32),
        pltpu.VMEM((LAYERS, C, H), jnp.bfloat16),
        pltpu.VMEM((LAYERS, H, C), jnp.bfloat16),
    )
    handed = pl.pallas_call(
        kernel,
        out_shape=kept,
        in_specs=[pl.BlockSpec(memory_space=pl.ANY)] * 6,
        out_specs=[pl.BlockSpec(memory_space=pltpu.VMEM)] * len(kept),
        scratch_shapes=[
            pltpu.VMEM((3 * ROWS, LON + 32, C), jnp.bfloat16),
            pltpu.VMEM((3 * ROWS, LON + 32, C), jnp.bfloat16),
            pltpu.VMEM((LAYERS, ROWS, PAD + LON + 64, C), jnp.float32),
            pltpu.VMEM((2, TAPS, LAYERS, C), jnp.bfloat16),
            pltpu.VMEM((TAPS, LAYERS, C), jnp.float32),
            pltpu.VMEM((ROWS, LON, C), jnp.bfloat16),
            pltpu.VMEM((ROWS, LON, C), jnp.bfloat16),
            pltpu.SemaphoreType.DMA((LAYERS, 2)),
            pltpu.SemaphoreType.DMA((len(SENT[0]),)),
            pltpu.SemaphoreType.DMA((len(SENT[1]),)),
            pltpu.SemaphoreType.DMA((5,)),
            pltpu.SemaphoreType.REGULAR((2,)),
            pltpu.SemaphoreType.DMA((6,)),
        ],
        compiler_params=pltpu.CompilerParams(collective_id=0, has_side_effects=True),
        name="step",
    )(fields, jnp.transpose(lat_taps, (1, 0, 2)), jnp.transpose(lon_taps, (1, 0, 2)), gains, w_in, w_out)
    handed = [pltpu.with_memory_space_constraint(array, pltpu.VMEM) for array in handed]
    return pl.pallas_call(
        finishing,
        out_shape=jax.ShapeDtypeStruct(fields.shape, fields.dtype),
        in_specs=[pl.BlockSpec(memory_space=pltpu.VMEM)] * len(kept),
        out_specs=pl.BlockSpec(memory_space=pl.ANY),
        scratch_shapes=[pltpu.VMEM((ROWS, TAIL_WIDTH, C), jnp.bfloat16), pltpu.SemaphoreType.DMA((4,))],
        compiler_params=pltpu.CompilerParams(vmem_limit_bytes=16 * 1024 * 1024),
        name="finishing",
    )(*handed)


def solution(mesh):
    return jax.shard_map(
        shards,
        mesh=mesh,
        in_specs=(P(("members", "section"), "band", None, None), P(), P(), P(), P(), P()),
        out_specs=P(("members", "section"), "band", None, None),
        check_vma=False,
    )
```
